32 devices in a mesh: rows: 16 (over z, y, x), cols: 2 (over core).
Axes of the slice: x: 2, y: 2, z: 4, core: 2. Of those that a mesh axis runs over, the one named last changes fastest.
Arguments:
- rhs: float32 [8192, 4096], P('rows', 'cols'), may hold values from -6 to 6
- leaf_v: float32 [8192, 256], P(('rows', 'cols')), may hold values from -8 to 8, as said below
- leaf_t: float32 [4096, 256], P('rows'), may hold values from -4 to 4, as said below
- merge_v: float32 [4, 4096, 256], P(None, 'rows'), may hold values from -4 to 4, as said below
- merge_t: float32 [4, 4096, 256], P(None, 'rows'), may hold values from -4 to 4, as said below
Outputs:
- applied: float32 [8192, 4096], P('rows', 'cols')
The draws below stay inside these ranges and needn't reach their ends.
Inputs may be any that keep to these rules, and one draw needn't show every extreme that they name: leaf_v block d is zero above its diagonal and one on it. leaf_t blocks are upper triangular. At level j, merge_v block d is the identity where bit log2(16) - 1 - j of d is 0, and upper triangular where it is 1. merge_t blocks are upper triangular, and at level j the blocks of devices d and d xor 2**(log2(16) - 1 - j) are equal.
All inputs are finite; a program needn't handle non-finite values.
Results may differ from the reference program's by a relative error of at most 0.0001.
Values sent between devices are 32-bit elements; how exact they have to be, the bound alone decides.
A program may use at most 64 MiB of HBM per device.

```python
import jax
import jax.numpy as jnp
from jax import lax

NB = 256
M_DEV = 512
LEVELS = 4
ROWS = 8192
K = 4096
N_ROWS = 16


def draw_leaf_v(key, part):
    shape = (M_DEV * N_ROWS, NB)
    base = jax.random.normal(key, shape, jnp.float32)
    row_pos = jnp.arange(M_DEV * N_ROWS, dtype=jnp.int32)[:, None] % M_DEV
    col_pos = jnp.arange(NB, dtype=jnp.int32)[None, :]
    below = jnp.where(row_pos > col_pos, base / jnp.sqrt(jnp.float32(M_DEV)), 0.0)
    return jnp.where(row_pos == col_pos, 1.0, below).astype(jnp.float32)


def upper_blocks(key, count, diag_lo, diag_hi, spread):
    shape = (count, NB, NB)
    base = jax.random.normal(jax.random.fold_in(key, 1), shape, jnp.float32)
    diagonal = jax.random.uniform(jax.random.fold_in(key, 2), shape, jnp.float32, diag_lo, diag_hi)
    row_pos = jnp.arange(NB, dtype=jnp.int32)[:, None]
    col_pos = jnp.arange(NB, dtype=jnp.int32)[None, :]
    above = jnp.where(row_pos < col_pos, base * (spread / jnp.sqrt(jnp.float32(NB))), 0.0)
    return jnp.where(row_pos == col_pos, diagonal, above)


def draw_leaf_t(key, part):
    return upper_blocks(key, N_ROWS, 0.5, 1.0, 0.5).reshape(N_ROWS * NB, NB)


def draw_merge_v(key, part):
    base = upper_blocks(key, LEVELS * N_ROWS, 0.6, 1.0, 0.7).reshape(LEVELS, N_ROWS, NB, NB)
    device_ids = jnp.arange(N_ROWS, dtype=jnp.int32)
    tree_depth = N_ROWS.bit_length() - 1
    identity = jnp.eye(NB, dtype=jnp.float32)
    layers = []
    for level_index in range(LEVELS):
        stride = 2 ** (tree_depth - 1 - level_index)
        upper_side = (device_ids // stride % 2 == 1)[:, None, None]
        layers.append(jnp.where(upper_side, base[level_index], identity[None, :, :]))
    return jnp.stack(layers).reshape(LEVELS, N_ROWS * NB, NB).astype(jnp.float32)


def draw_merge_t(key, part):
    base = upper_blocks(key, LEVELS * N_ROWS, 0.3, 0.6, 0.5).reshape(LEVELS, N_ROWS, NB, NB)
    device_ids = jnp.arange(N_ROWS, dtype=jnp.int32)
    tree_depth = N_ROWS.bit_length() - 1
    layers = []
    for level_index in range(LEVELS):
        stride = 2 ** (tree_depth - 1 - level_index)
        owner = device_ids // (2 * stride) * (2 * stride) + device_ids % stride
        layers.append(jnp.take(base[level_index], owner, axis=0))
    return jnp.stack(layers).reshape(LEVELS, N_ROWS * NB, NB)


def shard_levels(rng, shape, shards, least, high):
    level = 1.0
    for position, blocks in shards:
        steps = jax.random.uniform(jax.random.fold_in(jax.random.fold_in(rng, 6), position), (blocks,), jnp.float32, least / len(shards), high / len(shards))
        level = level * jnp.repeat(jnp.exp(steps), shape[position] // blocks).reshape((-1,) + (1,) * (len(shape) - 1 - position))
    return level


def noise(own_key, shape, deviation, most, pieces=(), kind=jnp.bfloat16):
    level = shard_levels(own_key, shape, pieces, -0.22, 0.18) if pieces else 1.0
    entries = jax.random.normal(own_key, shape, jnp.float32) * deviation * level
    return jnp.minimum(jnp.maximum(entries, -most), most).astype(kind)


def setup_inputs(seed: int = 0) -> dict:
    key_of = jax.random.split(jax.random.key(seed), 6)
    rhs = noise(key_of[0], (ROWS, K), 1.0, 6.0, ((0, 16), (1, 2)), jnp.float32)
    leaf_v = draw_leaf_v(jax.random.fold_in(key_of[5], 71), 0)
    leaf_t = draw_leaf_t(jax.random.fold_in(key_of[5], 71), 0)
    merge_v = draw_merge_v(jax.random.fold_in(key_of[5], 71), 0)
    merge_t = draw_merge_t(jax.random.fold_in(key_of[5], 71), 0)
    return {"rhs": rhs, "leaf_v": leaf_v, "leaf_t": leaf_t, "merge_v": merge_v, "merge_t": merge_t}


HIGH = lax.Precision.HIGHEST


def reference(rhs, leaf_v, leaf_t, merge_v, merge_t):
    blocks = rhs.reshape(N_ROWS, M_DEV, K)
    upper_rows = blocks[:, :NB]
    lower_rows = blocks[:, NB:]
    device_ids = jnp.arange(N_ROWS, dtype=jnp.int32)
    tree_depth = N_ROWS.bit_length() - 1
    for level_index in range(LEVELS):
        distance_bit = tree_depth - 1 - level_index
        partner_ids = jnp.bitwise_xor(device_ids, jnp.int32(2 ** distance_bit))
        merge_block = merge_v[level_index].reshape(N_ROWS, NB, NB)
        merge_tri = merge_t[level_index].reshape(N_ROWS, NB, NB)
        own_terms = jnp.einsum("dnk,dnj->dkj", merge_block, upper_rows, precision=HIGH)
        summed = own_terms + own_terms[partner_ids]
        weights = jnp.einsum("dkm,dmj->dkj", merge_tri, summed, precision=HIGH)
        upper_rows = upper_rows - jnp.einsum("dnk,dkj->dnj", merge_block, weights, precision=HIGH)
    stacked = jnp.concatenate([upper_rows, lower_rows], axis=1)
    leaf_blocks = leaf_v.reshape(N_ROWS, M_DEV, NB)
    leaf_tris = leaf_t.reshape(N_ROWS, NB, NB)

    def leaf_apply(items):
        block, refl, tri = items
        proj = jnp.dot(refl.T, block, precision=HIGH)
        inner = jnp.dot(tri, proj, precision=HIGH)
        return block - jnp.dot(refl, inner, precision=HIGH)

    result = lax.map(leaf_apply, (stacked, leaf_blocks, leaf_tris))
    return result.reshape(ROWS, K)
```

```python
import functools

import jax
import jax.numpy as jnp
from jax import lax
from jax.experimental import pallas as pl
from jax.experimental.pallas import tpu as pltpu
from jax.sharding import PartitionSpec as P

MESH = pl.DeviceIdType.MESH
WIDTH = 128
SINGLES = 4
OWN_LOOK = 4
FAR_LOOK = 3
LAG = 2


def halves(x):
    hi = x.astype(jnp.bfloat16)
    return hi, (x - hi.astype(jnp.float32)).astype(jnp.bfloat16)


def split(w):
    hi, lo = halves(w)
    return jnp.concatenate([hi, hi, lo], axis=1)


def times(w_ref, x):
    hi, lo = halves(x)
    return jnp.dot(w_ref[...], jnp.concatenate([hi, lo, hi], axis=0), preferred_element_type=jnp.float32)


def kernel(
    rhs, leaf_v, leaf_t, merge_v, merge_t, x,
    sent, got, mv, mt, lv, lt, far, v2, vt2, far_v2, far_vt2, l2, lt2,
    up_sem, low_sem, mv_sem, mt_sem, lv_sem, lt_sem, leaf_send, leaf_recv, far_send, far_recv, send_sem, recv_sem,
):
    levels, width = merge_v.shape[0], leaf_t.shape[1]
    chunks = x.shape[0]
    depth = lax.axis_size("rows").bit_length() - 1
    row, col = lax.axis_index("rows"), lax.axis_index("cols")
    partners, bits = [], []
    for j in range(levels):
        stride = 1 << (depth - 1 - j)
        bits.append((row // stride) % 2)
        partners.append(row + stride * (1 - 2 * bits[j]))
    beside = partners[1]
    across = partners[0] + partners[1] - row
    inner = bits[0] != bits[1]
    outer = bits[0] == bits[1]

    def columns(c):
        return pl.ds(pl.multiple_of(c * WIDTH, WIDTH), WIDTH)

    def upper_copy(c):
        return pltpu.make_async_copy(rhs.at[pl.ds(0, width), columns(c)], x.at[c, pl.ds(0, width)], up_sem.at[c])

    def lower_copy(c):
        low = pl.ds(width, x.shape[1] - width)
        return pltpu.make_async_copy(rhs.at[low, columns(c)], x.at[c, low], low_sem.at[c])

    def remote(src, slot, c, device):
        return pltpu.make_async_remote_copy(
            src_ref=src, dst_ref=got.at[slot, c],
            send_sem=send_sem.at[slot, c], recv_sem=recv_sem.at[slot, c],
            device_id=(device, col), device_id_type=MESH,
        )

    def cross(slot, c):
        return remote(sent.at[slot, c], slot, c, across)

    def hand_over(c):
        return remote(x.at[c, pl.ds(0, width)], 2, c, beside)

    def hand_back(c):
        return remote(sent.at[2, c], 2, c, beside)

    def exchange(j, c):
        return remote(sent.at[j + 1, c], j + 1, c, partners[j])

    half = leaf_v.shape[0]
    own_half = pl.ds(pl.multiple_of(col * half, half), half)
    leaf_here = pltpu.make_async_copy(leaf_v, lv.at[own_half], lv_sem)
    leaf_there = pltpu.make_async_remote_copy(
        src_ref=leaf_v, dst_ref=lv.at[own_half], send_sem=leaf_send, recv_sem=leaf_recv,
        device_id=(row, 1 - col), device_id_type=MESH,
    )
    mv_copies = [pltpu.make_async_copy(merge_v.at[j], mv.at[j], mv_sem.at[j]) for j in range(levels)]
    mt_copies = [pltpu.make_async_copy(merge_t.at[j], mt.at[j], mt_sem.at[j]) for j in range(levels)]
    lt_copy = pltpu.make_async_copy(leaf_t, lt, lt_sem)
    far_copies = [
        pltpu.make_async_remote_copy(
            src_ref=src, dst_ref=far.at[i], send_sem=far_send.at[i], recv_sem=far_recv.at[i],
            device_id=(beside, col), device_id_type=MESH,
        )
        for i, src in enumerate((merge_v.at[0], merge_t.at[0], merge_v.at[1]))
    ]

    mv_copies[0].start()
    barrier = pltpu.get_barrier_semaphore()
    for device in [across, beside] + partners[2:]:
        pl.semaphore_signal(barrier, inc=1, device_id=(device, col), device_id_type=MESH)
    pl.semaphore_signal(barrier, inc=1, device_id=(row, 1 - col), device_id_type=MESH)

    def load(c, carry):
        upper_copy(c).start()
        return carry

    def load_low(c, carry):
        lower_copy(c).start()
        return carry

    lax.fori_loop(0, chunks, load, 0)
    for j in range(levels):
        mt_copies[j].start()
        if j > 0:
            mv_copies[j].start()
    leaf_here.start()
    lt_copy.start()
    lax.fori_loop(0, chunks, load_low, 0)

    def prepare_v(j):
        mv_copies[j].wait()
        v = mv[j]
        vt2[j] = split(v.T)
        v2[j] = split(v)

    def prepare_t(j):
        mt_copies[j].wait()
        v2[j] = split(times(v2.at[j], mt[j]))

    def prepare_far(i):
        far_copies[i].wait_recv()
        if i == 1:
            far_v2[0] = split(times(far_v2.at[0], far[1]))
        else:
            v = far[i]
            far_vt2[i // 2] = split(v.T)
            far_v2[i // 2] = split(v)
            if i == 2:
                far_v2[1] = split(times(far_v2.at[1], mt[1]))

    singles = min(SINGLES, chunks)
    pairs = (chunks - singles) // 2
    units = pairs + chunks - 2 * pairs

    def read(ref, c, n):
        return jnp.concatenate([ref[c + i] for i in range(n)], axis=1)

    def write(ref, c, n, value):
        for i in range(n):
            ref[c + i] = value[:, i * WIDTH : (i + 1) * WIDTH]

    def read_upper(c, n):
        return jnp.concatenate([x[c + i, :width] for i in range(n)], axis=1)

    def write_upper(c, n, value):
        for i in range(n):
            x[c + i, :width] = value[:, i * WIDTH : (i + 1) * WIDTH]

    def on_unit(stage, u, take):
        take = take & (u >= 0) & (u < units)

        @pl.when(take & (u < pairs))
        def _():
            stage(2 * u, 2)

        @pl.when(take & (u >= pairs))
        def _():
            stage(pairs + u, 1)

    def first_own(c, n):
        for i in range(n):
            upper_copy(c + i).wait()
        write(sent.at[0], c, n, times(vt2.at[0], read_upper(c, n)))
        for i in range(n):
            cross(0, c + i).start()

    def first_far(c, n):
        for i in range(n):
            hand_back(c + i).wait_recv()
        write(sent.at[1], c, n, times(far_vt2.at[0], read(got.at[2], c, n)))
        for i in range(n):
            cross(1, c + i).start()

    prepare_v(0)
    pl.semaphore_wait(barrier, levels + 1)

    def give(c, carry):
        upper_copy(c).wait()
        hand_over(c).start()
        return carry

    @pl.when(outer)
    def _():
        far_copies[0].start()
        give(0, 0)
        give(1, 0)
        far_copies[1].start()
        give(2, 0)
        give(3, 0)
        far_copies[2].start()
        lax.fori_loop(4, chunks, give, 0)

    @pl.when(inner)
    def _():
        for u in range(OWN_LOOK):
            first_own(2 * u, 2)

    leaf_there.start()
    prepare_t(0)
    for j in range(1, levels):
        prepare_v(j)
        prepare_t(j)
    leaf_here.wait()
    lt_copy.wait()

    @pl.when(inner)
    def _():
        prepare_far(0)
        for u in range(FAR_LOOK):
            first_far(2 * u, 2)
        prepare_far(1)
        prepare_far(2)

    leaf_there.wait()
    whole = lv[...]
    l2[...] = split(whole)
    l2[...] = split(times(l2, lt[...]))
    lt2[...] = split(whole.T)

    def send_on(j, c, n, upper):
        write_upper(c, n, upper)
        write(sent.at[j + 1], c, n, times(vt2.at[j], upper))
        for i in range(n):
            exchange(j, c + i).start()

    def two_levels(c, n):
        for i in range(n):
            cross(0, c + i).wait_recv()
            cross(1, c + i).wait_recv()
        far_sum = read(sent.at[1], c, n) + read(got.at[0], c, n)
        own_sum = read(sent.at[0], c, n) + read(got.at[1], c, n)
        far_u = read(got.at[2], c, n) - times(far_v2.at[0], far_sum)
        own_u = read_upper(c, n) - times(v2.at[0], own_sum)
        both = times(vt2.at[1], own_u) + times(far_vt2.at[1], far_u)
        write(sent.at[2], c, n, far_u - times(far_v2.at[1], both))
        for i in range(n):
            hand_back(c + i).start()
        send_on(2, c, n, own_u - times(v2.at[1], both))

    def take_back(c, n):
        for i in range(n):
            hand_over(c + i).wait()
        send_on(2, c, n, read(got.at[2], c, n))

    def merged(j, c, n):
        for i in range(n):
            exchange(j, c + i).wait_recv()
        return read_upper(c, n) - times(v2.at[j], read(sent.at[j + 1], c, n) + read(got.at[j + 1], c, n))

    def middle(j, c, n):
        send_on(j + 1, c, n, merged(j, c, n))

    def last(c, n):
        for i in range(n):
            lower_copy(c + i).wait()
        write_upper(c, n, merged(levels - 1, c, n))
        block = read(x, c, n)
        write(x, c, n, block - times(l2, times(lt2, block)))

    def step(t, carry):
        on_unit(first_own, t + OWN_LOOK, inner)
        on_unit(first_far, t + FAR_LOOK, inner)
        for j in reversed(range(2, levels)):
            stage = last if j == levels - 1 else functools.partial(middle, j)
            on_unit(stage, t - (j - 1) * LAG, True)
        on_unit(two_levels, t, inner)
        on_unit(take_back, t, outer)
        return carry

    lax.fori_loop(0, units + (levels - 2) * LAG, step, 0)

    def drain(c, carry):
        for j in range(2, levels):
            exchange(j, c).wait_send()
        return carry

    def drain_inner(c, carry):
        cross(0, c).wait_send()
        cross(1, c).wait_send()
        hand_back(c).wait_send()
        return carry

    @pl.when(inner)
    def _():
        lax.fori_loop(0, chunks, drain_inner, 0)

    @pl.when(outer)
    def _():
        for copy in far_copies:
            copy.wait_send()

    lax.fori_loop(0, chunks, drain, 0)


def store(x, out, sem):
    copies = [
        pltpu.make_async_copy(x.at[c], out.at[:, pl.ds(c * WIDTH, WIDTH)], sem.at[c]) for c in range(x.shape[0])
    ]
    for copy in copies:
        copy.start()
    for copy in copies:
        copy.wait()


def body(rhs, leaf_v, leaf_t, merge_v, merge_t):
    rows, cols = rhs.shape
    levels, width = merge_v.shape[0], leaf_t.shape[1]
    chunks = cols // WIDTH
    f32, bf16 = jnp.float32, jnp.bfloat16
    dma = pltpu.SemaphoreType.DMA
    anywhere = pl.BlockSpec(memory_space=pltpu.HBM)
    x = pl.pallas_call(
        kernel,
        out_shape=pltpu.VMEM((chunks, rows, WIDTH), f32),
        in_specs=[anywhere] * 5,
        out_specs=pl.BlockSpec(memory_space=pltpu.VMEM),
        scratch_shapes=[
            pltpu.VMEM((levels + 1, chunks, width, WIDTH), f32),
            pltpu.VMEM((levels + 1, chunks, width, WIDTH), f32),
            pltpu.VMEM((levels, width, width), f32),
            pltpu.VMEM((levels, width, width), f32),
            pltpu.VMEM((rows, width), f32),
            pltpu.VMEM((width, width), f32),
            pltpu.VMEM((3, width, width), f32),
            pltpu.VMEM((levels, width, 3 * width), bf16),
            pltpu.VMEM((levels, width, 3 * width), bf16),
            pltpu.VMEM((2, width, 3 * width), bf16),
            pltpu.VMEM((2, width, 3 * width), bf16),
            pltpu.VMEM((rows, 3 * width), bf16),
            pltpu.VMEM((width, 3 * rows), bf16),
            dma((chunks,)),
            dma((chunks,)),
            dma((levels,)),
            dma((levels,)),
            dma,
            dma,
            dma,
            dma,
            dma((3,)),
            dma((3,)),
            dma((levels + 1, chunks)),
            dma((levels + 1, chunks)),
        ],
        compiler_params=pltpu.CompilerParams(
            collective_id=0, has_side_effects=True, vmem_limit_bytes=52 * 1024 * 1024
        ),
    )(rhs, leaf_v, leaf_t, merge_v, merge_t)
    return pl.pallas_call(
        store,
        out_shape=jax.ShapeDtypeStruct((rows, cols), f32),
        in_specs=[pl.BlockSpec(memory_space=pltpu.VMEM)],
        out_specs=anywhere,
        scratch_shapes=[dma((chunks,))],
        compiler_params=pltpu.CompilerParams(vmem_limit_bytes=4 * 1024 * 1024),
    )(pltpu.with_memory_space_constraint(x, pltpu.VMEM))


def solution(mesh):
    return jax.shard_map(
        body,
        mesh=mesh,
        in_specs=(
            P("rows", "cols"),
            P(("rows", "cols"), None),
            P("rows", None),
            P(None, "rows", None),
            P(None, "rows", None),
        ),
        out_specs=P("rows", "cols"),
        check_vma=False,
    )
```

```python
import jax
import jax.numpy as jnp
from jax import lax
from jax.experimental import pallas as pl
from jax.experimental.pallas import tpu as pltpu
from jax.sharding import PartitionSpec as P

MESH = pl.DeviceIdType.MESH
WIDTH = 128
TAIL = ((128, 128), (128, 128), (64, 64, 64, 64))
OWN_LOOK = 4
FAR_LOOK = 2
LAG = 2
INNER = (
    ("merge", -2), ("leaf", -2), ("settle", 0), ("merge", -1), ("leaf", -1), ("base", 2),
    ("settle", 1), ("settle", 2), ("merge", 1), ("last", -1), ("merge", 0), ("settle", 3),
    ("settle", 4), ("settle", 5), ("merge", 2), ("settle", 6), ("merge", 3), ("settle", 7),
    ("merge", 5), ("merge", 6), ("last", -2), ("leaf", 1), ("merge", 7), ("merge", 4),
    ("last", -4), ("leaf", 2), ("leaf", 0), ("last", 1), ("last", 0), ("last", -3),
    ("last", 2),
)
OUTER = (
    ("settle", 0), ("merge", -2), ("settle", 1), ("merge", -1), ("leaf", -1), ("last", -3),
    ("settle", 2), ("leaf", -2), ("merge", 0), ("merge", 1), ("base", 2), ("last", -4),
    ("merge", 2), ("settle", 3), ("last", -1), ("leaf", 0), ("settle", 5), ("settle", 4),
    ("last", 0), ("merge", 3), ("settle", 6), ("leaf", 1), ("settle", 7), ("merge", 5),
    ("merge", 4), ("last", 1), ("merge", 6), ("merge", 7), ("leaf", 2), ("last", -2),
    ("last", 2),
)


def halves(x):
    hi = x.astype(jnp.bfloat16)
    return hi, (x - hi.astype(jnp.float32)).astype(jnp.bfloat16)


def split(w):
    hi, lo = halves(w)
    return jnp.concatenate([hi, hi, lo], axis=1)


def unsplit(w):
    n = w.shape[1] // 3
    return w[:, :n].astype(jnp.float32) + w[:, 2 * n :].astype(jnp.float32)


def stacked(x):
    hi, lo = halves(x)
    return jnp.concatenate([hi, lo, hi], axis=0)


def product(w, x):
    return jnp.dot(w, stacked(x), preferred_element_type=jnp.float32)


def times(w_ref, x):
    return product(w_ref[...], x)


def pack(v, w):
    rows = v.shape[0] * w // WIDTH
    return jnp.concatenate([v[i * rows : (i + 1) * rows] for i in range(WIDTH // w)], axis=1)


def unpack(v, w):
    return jnp.concatenate([v[:, i * w : (i + 1) * w] for i in range(WIDTH // w)], axis=0)


class Wide:
    def __init__(self, c, n, x, width):
        self.c, self.n, self.x, self.width = c, n, x, width
        self.chunks = [c + i for i in range(n)]
        self.parts = [(c + i, c + i, None) for i in range(n)]

    def read(self, ref):
        return jnp.concatenate([ref[c] for c in self.chunks], axis=1)

    def write(self, ref, value):
        for i, c in enumerate(self.chunks):
            ref[c] = value[:, i * WIDTH : (i + 1) * WIDTH]

    read_whole = read

    def read_upper(self):
        return jnp.concatenate([self.x[c, : self.width] for c in self.chunks], axis=1)

    def write_upper(self, value):
        for i, c in enumerate(self.chunks):
            self.x[c, : self.width] = value[:, i * WIDTH : (i + 1) * WIDTH]

    def read_block(self):
        return self.read(self.x)

    def write_block(self, value):
        self.write(self.x, value)


class Piece:
    def __init__(self, c, index, o, w, x, width):
        self.c, self.o, self.w, self.x, self.width = c, o, w, x, width
        self.chunks = [c]
        per = width // WIDTH
        self.rows = slice(o * per, (o + w) * per)
        self.parts = [(c, index, pl.ds(o * per, w * per))]

    def read(self, ref):
        return unpack(ref[self.c, self.rows], self.w)

    def write(self, ref, value):
        ref[self.c, self.rows] = pack(value, self.w)

    def read_upper(self):
        return self.x[self.c, : self.width, self.o : self.o + self.w]

    def write_upper(self, value):
        self.x[self.c, : self.width, self.o : self.o + self.w] = value

    def read_block(self):
        return self.x[self.c, :, self.o : self.o + self.w]

    def write_block(self, value):
        self.x[self.c, :, self.o : self.o + self.w] = value


class Whole(Wide):
    def __init__(self, pieces, x, width):
        super().__init__(pieces[0].c, 1, x, width)
        self.pieces = pieces
        self.parts = [part for piece in pieces for part in piece.parts]

    def read(self, ref):
        return jnp.concatenate([piece.read(ref) for piece in self.pieces], axis=1)

    def write(self, ref, value):
        for p in self.pieces:
            p.write(ref, value[:, p.o : p.o + p.w])

    def read_whole(self, ref):
        return ref[self.c]

    def read_block(self):
        return self.x[self.c]

    def write_block(self, value):
        self.x[self.c] = value


class Group:
    def __init__(self, first, second):
        self.members = (first, second)
        self.chunks = first.chunks + second.chunks
        self.parts = first.parts + second.parts

    def both(self, name, *args):
        return jnp.concatenate([getattr(m, name)(*args) for m in self.members], axis=1)

    def each(self, name, value, *args):
        half = value.shape[1] // 2
        for i, m in enumerate(self.members):
            getattr(m, name)(*args, value[:, i * half : (i + 1) * half])

    def read(self, ref):
        return self.both("read", ref)

    def write(self, ref, value):
        self.each("write", value, ref)

    def read_whole(self, ref):
        return self.both("read_whole", ref)

    def read_upper(self):
        return self.both("read_upper")

    def write_upper(self, value):
        self.each("write_upper", value)

    def read_block(self):
        return self.both("read_block")

    def write_block(self, value):
        self.each("write_block", value)


def kernel(
    rhs, leaf_v, leaf_t, merge_v, merge_t, x,
    sent, got, mv, mt, lv, lt, far, v2, vt2, far_v2, far_vt2, l2, lt2, base_w, cross_w, merge_w, leaf_w,
    up_sem, low_sem, mv_sem, mt_sem, lv_sem, lt_sem, leaf_send, leaf_recv, far_send, far_recv, send_sem, recv_sem,
):
    levels, width = merge_v.shape[0], leaf_t.shape[1]
    chunks = x.shape[0]
    depth = lax.axis_size("rows").bit_length() - 1
    row, col = lax.axis_index("rows"), lax.axis_index("cols")
    partners, bits = [], []
    for j in range(levels):
        stride = 1 << (depth - 1 - j)
        bits.append((row // stride) % 2)
        partners.append(row + stride * (1 - 2 * bits[j]))
    beside = partners[1]
    across = partners[0] + partners[1] - row
    inner = bits[0] != bits[1]
    outer = bits[0] == bits[1]

    def columns(c):
        return pl.ds(pl.multiple_of(c * WIDTH, WIDTH), WIDTH)

    def upper_copy(c):
        return pltpu.make_async_copy(rhs.at[pl.ds(0, width), columns(c)], x.at[c, pl.ds(0, width)], up_sem.at[c])

    def lower_copy(c):
        low = pl.ds(width, x.shape[1] - width)
        return pltpu.make_async_copy(rhs.at[low, columns(c)], x.at[c, low], low_sem.at[c])

    def remote(src, dst, slot, index, device):
        return pltpu.make_async_remote_copy(
            src_ref=src, dst_ref=dst, send_sem=send_sem.at[slot, index], recv_sem=recv_sem.at[slot, index],
            device_id=(device, col), device_id_type=MESH,
        )

    def move(slot, part, device):
        c, index, rows = part
        if rows is None:
            return remote(sent.at[slot, c], got.at[slot, c], slot, index, device)
        return remote(sent.at[slot, c, rows], got.at[slot, c, rows], slot, index, device)

    def cross(slot, part):
        return move(slot, part, across)

    def hand_over(c):
        return remote(x.at[c, pl.ds(0, width)], got.at[2, c], 2, c, beside)

    def hand_back(part):
        return move(2, part, beside)

    def exchange(j, part):
        return move(j + 1, part, partners[j])

    half = leaf_v.shape[0]
    own_half = pl.ds(pl.multiple_of(col * half, half), half)
    leaf_here = pltpu.make_async_copy(leaf_v, lv.at[own_half], lv_sem)
    leaf_there = pltpu.make_async_remote_copy(
        src_ref=leaf_v, dst_ref=lv.at[own_half], send_sem=leaf_send, recv_sem=leaf_recv,
        device_id=(row, 1 - col), device_id_type=MESH,
    )
    mv_copies = [pltpu.make_async_copy(merge_v.at[j], mv.at[j], mv_sem.at[j]) for j in range(levels)]
    mt_copies = [pltpu.make_async_copy(merge_t.at[j], mt.at[j], mt_sem.at[j]) for j in range(levels)]
    lt_copy = pltpu.make_async_copy(leaf_t, lt, lt_sem)
    share = width // lax.axis_size("cols")
    own_share = pl.ds(pl.multiple_of(col * share, share), share)
    far_copies = [
        pltpu.make_async_remote_copy(
            src_ref=src, dst_ref=far.at[i, own_share], send_sem=far_send.at[i], recv_sem=far_recv.at[i],
            device_id=(beside, col), device_id_type=MESH,
        )
        for i, src in enumerate((merge_v.at[0, own_share], merge_t.at[0, own_share], merge_v.at[1, own_share]))
    ]
    pass_on = [
        pltpu.make_async_remote_copy(
            src_ref=far.at[i, own_share], dst_ref=far.at[i, own_share], send_sem=far_send.at[3 + i],
            recv_sem=far_recv.at[3 + i], device_id=(row, 1 - col), device_id_type=MESH,
        )
        for i in range(3)
    ]

    mv_copies[0].start()
    barrier = pltpu.get_barrier_semaphore()
    for device in [across, beside] + partners[2:]:
        pl.semaphore_signal(barrier, inc=1, device_id=(device, col), device_id_type=MESH)
    pl.semaphore_signal(barrier, inc=1, device_id=(row, 1 - col), device_id_type=MESH)

    def load(c, carry):
        upper_copy(c).start()
        return carry

    def load_low(c, carry):
        lower_copy(c).start()
        return carry

    lax.fori_loop(0, chunks, load, 0)
    for j in range(levels):
        mt_copies[j].start()
        if j > 0:
            mv_copies[j].start()
    leaf_here.start()
    lt_copy.start()
    lax.fori_loop(0, chunks, load_low, 0)

    def prepare_v(j):
        mv_copies[j].wait()
        v = mv[j]
        vt2[j] = split(v.T)
        v2[j] = split(v)

    def prepare_t(j):
        mt_copies[j].wait()
        mv[j] = times(v2.at[j], mt[j])
        v2[j] = split(mv[j])

    def prepare_far(i):
        far_copies[i].wait_recv()
        pass_on[i].start()
        pass_on[i].wait()
        if i == 1:
            far[0] = times(far_v2.at[0], far[1])
            far_v2[0] = split(far[0])
        else:
            v = far[i]
            far_vt2[i // 2] = split(v.T)
            far_v2[i // 2] = split(v)
            if i == 2:
                far_v2[1] = split(times(far_v2.at[1], mt[1]))

    def prepare_cross():
        eye = jnp.eye(width, dtype=jnp.float32)
        onward = jnp.concatenate([unsplit(far_vt2[1]), unsplit(vt2[1])], axis=1)
        back, here = times(far_v2.at[1], onward), times(v2.at[1], onward)
        back = jnp.concatenate([eye - back[:, :width], -back[:, width:]], axis=1)
        here = jnp.concatenate([-here[:, :width], eye - here[:, width:]], axis=1)
        for i, w in enumerate((back, times(vt2.at[2], here), here)):
            base_w[i] = split(w)
            cross_w[i] = split(
                jnp.concatenate(
                    [product(split(w[:, :width]), far[0]), product(split(w[:, width:]), mv[0])], axis=1
                )
            )

    def prepare_merge(j):
        merge_w[j - 2, :width] = split(times(vt2.at[j + 1], mv[j]))
        merge_w[j - 2, width:] = v2[j]

    def prepare_leaf():
        whole = lv[...]
        l2[...] = split(whole)
        l2[...] = split(times(l2, lt[...]))
        lt2[...] = split(whole.T)
        last = jnp.concatenate([mv[levels - 1], jnp.zeros((whole.shape[0] - width, width), jnp.float32)], axis=0)
        leaf_w[...] = split(last - times(l2, times(lt2, last)))

    pairs = chunks // 2 - len(TAIL)

    def pair(u):
        return Wide(2 * u, 2, x, width)

    units, groups, c = [], [], 2 * pairs
    index = chunks
    for widths in TAIL:
        members, column, pieces = [], 0, []
        for w in widths:
            if w == WIDTH:
                members.append(Wide(c, 1, x, width))
                units.append(members[-1])
                c += 1
                continue
            pieces.append(Piece(c, index, column, w, x, width))
            units.append(pieces[-1])
            index += 1
            column += w
            if column == WIDTH:
                members.append(Whole(pieces, x, width))
                column, pieces = 0, []
                c += 1
        groups.append(Group(*members))

    def on_pair(stage, u, take):
        @pl.when(take & (u >= 0) & (u < pairs))
        def _():
            stage(pair(u))

    def first_own(u, together=False):
        for c in u.chunks:
            upper_copy(c).wait()
        u.write(sent.at[0], times(vt2.at[0], u.read_upper()))
        if not together:
            for part in u.parts:
                cross(0, part).start()

    def first_far(u, together=False):
        for c in u.chunks:
            hand_over(c).wait_recv()
        u.write(sent.at[1], times(far_vt2.at[0], u.read_whole(got.at[2])))
        for part in u.parts:
            if together:
                cross(0, part).start()
            cross(1, part).start()

    def before_cross(u):
        news = stacked(jnp.concatenate([u.read_whole(got.at[2]), u.read_upper()], axis=0))
        for i, write in enumerate((lambda v: u.write(sent.at[2], v), lambda v: u.write(sent.at[3], v), u.write_upper)):
            write(jnp.dot(base_w[i], news, preferred_element_type=jnp.float32))

    prepare_v(0)
    pl.semaphore_wait(barrier, levels + 1)

    def give(c, carry):
        upper_copy(c).wait()
        hand_over(c).start()
        return carry

    @pl.when(outer)
    def _():
        far_copies[0].start()
        lax.fori_loop(0, 4, give, 0)
        far_copies[1].start()
        far_copies[2].start()
        lax.fori_loop(4, chunks, give, 0)

    @pl.when(inner)
    def _():
        first_own(pair(0))
        first_own(pair(1))

    leaf_there.start()
    prepare_t(0)
    for j in range(1, levels):
        prepare_v(j)
        prepare_t(j)
    for j in range(2, levels - 1):
        prepare_merge(j)
    leaf_here.wait()
    lt_copy.wait()
    leaf_there.wait()
    prepare_leaf()

    def first_both(u):
        first_own(u, True)
        first_far(u, True)

    @pl.when(inner)
    def _():
        prepare_far(0)
        first_far(pair(0))
        first_own(pair(2))
        first_far(pair(1))
        first_own(pair(3))
        prepare_far(1)
        prepare_far(2)
        prepare_cross()
        before_cross(pair(0))

    def before_merge(j, u):
        if j < levels - 1:
            u.write(sent.at[j + 2], times(vt2.at[j + 1], u.read_upper()))
        else:
            for c in u.chunks:
                lower_copy(c).wait()
            block = u.read_block()
            u.write_block(block - times(l2, times(lt2, block)))

    def crossed(u):
        for part in u.parts:
            cross(0, part).wait_recv()
            cross(1, part).wait_recv()
        far_sum, own_sum = u.read(sent.at[1]) + u.read(got.at[0]), u.read(sent.at[0]) + u.read(got.at[1])
        news = stacked(jnp.concatenate([far_sum, own_sum], axis=0))

        def add(i):
            return jnp.dot(cross_w[i], news, preferred_element_type=jnp.float32)

        u.write(sent.at[2], u.read(sent.at[2]) - add(0))
        for part in u.parts:
            hand_back(part).start()
        u.write(sent.at[3], u.read(sent.at[3]) - add(1))
        for part in u.parts:
            exchange(2, part).start()
        u.write_upper(u.read_upper() - add(2))

    def take_back(u):
        if not isinstance(u, Piece):
            for c in u.chunks:
                hand_over(c).wait_send()
        for part in u.parts:
            hand_back(part).wait_recv()
        upper = u.read(got.at[2])
        u.write(sent.at[3], times(vt2.at[2], upper))
        for part in u.parts:
            exchange(2, part).start()
        u.write_upper(upper)

    def merge(j, u):
        for part in u.parts:
            exchange(j, part).wait_recv()
        news = u.read(sent.at[j + 1]) + u.read(got.at[j + 1])
        if j == levels - 1:
            u.write_block(u.read_block() - times(leaf_w, news))
            return
        delta = product(merge_w[j - 2], news)
        u.write(sent.at[j + 2], u.read(sent.at[j + 2]) - delta[:width])
        for part in u.parts:
            exchange(j + 1, part).start()
        u.write_upper(u.read_upper() - delta[width:])

    def merge_stage(j):
        def stage(u):
            merge(j, u)
            if j < levels - 1:
                before_merge(j + 1, u)

        return stage

    def enter(u):
        before_merge(2, u)

    def step(t, carry):
        on_pair(first_far, t + FAR_LOOK, inner)
        for i, group in enumerate(groups[:FAR_LOOK]):

            @pl.when(inner & (t + FAR_LOOK == pairs + i))
            def _():
                first_both(group)

        on_pair(first_own, t + OWN_LOOK, inner)
        on_pair(before_cross, t + 1, inner)

        @pl.when(inner & (t + 1 == pairs))
        def _():
            for group in groups[:-1]:
                before_cross(group)

        for j in reversed(range(2, levels)):
            on_pair(merge_stage(j), t - (j - 1) * LAG, True)
        on_pair(crossed, t, inner)
        on_pair(take_back, t, outer)
        on_pair(enter, t, True)
        return carry

    lax.fori_loop(0, pairs, step, 0)

    def finish(order, settle):
        for what, i in order:
            unit = units[i] if i >= 0 else pair(pairs + i)
            if what == "base":
                if settle is crossed:
                    before_cross(groups[i])
                continue
            if what == "settle":
                settle(unit)
                enter(unit)
                continue
            if what == "merge":
                merge(2, unit)
                continue
            group = groups[i] if i >= 0 else pair(pairs + i)
            if what == "leaf":
                before_merge(levels - 1, group)
            else:
                merge(levels - 1, group)

    @pl.when(inner)
    def _():
        for group in groups[FAR_LOOK:]:
            first_both(group)
        finish(INNER, crossed)

    @pl.when(outer)
    def _():
        for c in sorted(set(u.c for u in units if isinstance(u, Piece))):
            hand_over(c).wait_send()
        finish(OUTER, take_back)

    every = [part for u in units for part in u.parts]

    def drain(part):
        for j in range(2, levels):
            exchange(j, part).wait_send()

    def drain_inner(part):
        cross(0, part).wait_send()
        cross(1, part).wait_send()
        hand_back(part).wait_send()

    def over_wide(stage):
        def one(c, carry):
            stage((c, c, None))
            return carry

        lax.fori_loop(0, 2 * pairs, one, 0)
        for part in every:
            stage(part)

    @pl.when(inner)
    def _():
        over_wide(drain_inner)

    @pl.when(outer)
    def _():
        for copy in far_copies:
            copy.wait_send()

    over_wide(drain)


def store(x, out, sem):
    copies = [
        pltpu.make_async_copy(x.at[c], out.at[:, pl.ds(c * WIDTH, WIDTH)], sem.at[c]) for c in range(x.shape[0])
    ]
    for copy in copies:
        copy.start()
    for copy in copies:
        copy.wait()


def body(rhs, leaf_v, leaf_t, merge_v, merge_t):
    rows, cols = rhs.shape
    levels, width = merge_v.shape[0], leaf_t.shape[1]
    chunks = cols // WIDTH
    indices = chunks + sum(w < WIDTH for widths in TAIL for w in widths)
    f32, bf16 = jnp.float32, jnp.bfloat16
    dma = pltpu.SemaphoreType.DMA
    anywhere = pl.BlockSpec(memory_space=pltpu.HBM)
    x = pl.pallas_call(
        kernel,
        out_shape=pltpu.VMEM((chunks, rows, WIDTH), f32),
        in_specs=[anywhere] * 5,
        out_specs=pl.BlockSpec(memory_space=pltpu.VMEM),
        scratch_shapes=[
            pltpu.VMEM((levels + 1, chunks, width, WIDTH), f32),
            pltpu.VMEM((levels + 1, chunks, width, WIDTH), f32),
            pltpu.VMEM((levels, width, width), f32),
            pltpu.VMEM((levels, width, width), f32),
            pltpu.VMEM((rows, width), f32),
            pltpu.VMEM((width, width), f32),
            pltpu.VMEM((3, width, width), f32),
            pltpu.VMEM((levels, width, 3 * width), bf16),
            pltpu.VMEM((levels, width, 3 * width), bf16),
            pltpu.VMEM((2, width, 3 * width), bf16),
            pltpu.VMEM((2, width, 3 * width), bf16),
            pltpu.VMEM((rows, 3 * width), bf16),
            pltpu.VMEM((width, 3 * rows), bf16),
            pltpu.VMEM((3, width, 6 * width), bf16),
            pltpu.VMEM((3, width, 6 * width), bf16),
            pltpu.VMEM((levels - 3, 2 * width, 3 * width), bf16),
            pltpu.VMEM((rows, 3 * width), bf16),
            dma((chunks,)),
            dma((chunks,)),
            dma((levels,)),
            dma((levels,)),
            dma,
            dma,
            dma,
            dma,
            dma((6,)),
            dma((6,)),
            dma((levels + 1, indices)),
            dma((levels + 1, indices)),
        ],
        compiler_params=pltpu.CompilerParams(
            collective_id=0, has_side_effects=True, vmem_limit_bytes=52 * 1024 * 1024
        ),
    )(rhs, leaf_v, leaf_t, merge_v, merge_t)
    return pl.pallas_call(
        store,
        out_shape=jax.ShapeDtypeStruct((rows, cols), f32),
        in_specs=[pl.BlockSpec(memory_space=pltpu.VMEM)],
        out_specs=anywhere,
        scratch_shapes=[dma((chunks,))],
        compiler_params=pltpu.CompilerParams(vmem_limit_bytes=4 * 1024 * 1024),
    )(pltpu.with_memory_space_constraint(x, pltpu.VMEM))


def solution(mesh):
    return jax.shard_map(
        body,
        mesh=mesh,
        in_specs=(
            P("rows", "cols"),
            P(("rows", "cols"), None),
            P("rows", None),
            P(None, "rows", None),
            P(None, "rows", None),
        ),
        out_specs=P("rows", "cols"),
        check_vma=False,
    )
```

```python
import jax
import jax.numpy as jnp
from jax import lax
from jax.experimental import pallas as pl
from jax.experimental.pallas import tpu as pltpu
from jax.sharding import PartitionSpec as P

MESH = pl.DeviceIdType.MESH
WIDTH = 128
PIECE = 64
PER = 4
OWN_LOOK = 4
FAR_LOOK = 2
LAG = 2
STEP = 8192
OPS = ("own", "far", "base", "settle", "merge", "leaf", "last", "ready", "near", "rest")
TAIL = ((128, 128), (128, 128), (64, 64, 64, 64))
INNER = (
    ("merge", -2), ("leaf", -2), ("settle", 0), ("merge", -1), ("leaf", -1), ("base", 2),
    ("settle", 1), ("settle", 2), ("merge", 1), ("last", -1), ("merge", 0), ("settle", 3),
    ("settle", 4), ("settle", 5), ("merge", 2), ("settle", 6), ("merge", 3), ("settle", 7),
    ("merge", 5), ("merge", 6), ("last", -2), ("leaf", 1), ("merge", 7), ("merge", 4),
    ("last", -4), ("leaf", 2), ("leaf", 0), ("last", 1), ("last", 0), ("last", -3),
    ("last", 2),
)
OUTER = (
    ("settle", 0), ("merge", -2), ("settle", 1), ("merge", -1), ("leaf", -1), ("last", -3),
    ("settle", 2), ("leaf", -2), ("merge", 0), ("merge", 1), ("last", -4), ("merge", 2),
    ("settle", 3), ("last", -1), ("leaf", 0), ("settle", 5), ("settle", 4), ("last", 0),
    ("merge", 3), ("settle", 6), ("leaf", 1), ("settle", 7), ("merge", 5), ("merge", 4),
    ("last", 1), ("merge", 6), ("merge", 7), ("leaf", 2), ("last", -2), ("last", 2),
)

def halves(x):
    hi = x.astype(jnp.bfloat16)
    return hi, (x - hi.astype(jnp.float32)).astype(jnp.bfloat16)


def split(w):
    hi, lo = halves(w)
    return jnp.concatenate([hi, hi, lo], axis=1)


def unsplit(w):
    n = w.shape[1] // 3
    return w[:, :n].astype(jnp.float32) + w[:, 2 * n :].astype(jnp.float32)


def stacked(x):
    hi, lo = halves(x)
    return jnp.concatenate([hi, lo, hi], axis=0)


def product(w, x):
    return jnp.dot(w, stacked(x), preferred_element_type=jnp.float32)


def times(w_ref, x):
    return product(w_ref[...], x)


def swap(a, b):
    left = lax.broadcasted_iota(jnp.int32, a.shape, 1) < PIECE
    return (
        jnp.where(left, a, pltpu.roll(b, PIECE, 1)),
        jnp.where(left, pltpu.roll(a, PIECE, 1), b),
    )


def unpack(pieces):
    columns = [jnp.concatenate(swap(pieces[i], pieces[i + 1]), axis=0) for i in range(0, PER, 2)]
    return jnp.concatenate(columns, axis=1)


def pack(value):
    rows = value.shape[0] // 2
    pieces = []
    for i in range(PER // 2):
        part = value[:, i * WIDTH : (i + 1) * WIDTH]
        pieces += swap(part[:rows], part[rows:])
    return pieces


def schedule(pairs):
    starts, at = [], pairs * PER
    for widths in TAIL:
        for w in widths:
            starts.append((at, w // PIECE))
            at += w // PIECE

    def unit(i):
        return starts[i] if i >= 0 else ((pairs + i) * PER, PER)

    count = pairs + len(TAIL)
    inner = [("own", 0, 1), ("own", 1, 1), ("ready", 0, 0), ("near", 0, 0), ("far", 0, 0), ("own", 2, 1), ("far", 1, 0)]
    inner += [("own", 3, 1), ("rest", 0, 0), ("base", 0, 0)]
    outer = [("ready", 0, 0)]

    def far(k):
        if k < pairs:
            return [("far", k, 0)]
        return [("own", k, 0), ("far", k, 1)] if k < count else []

    for t in range(pairs):
        inner += far(t + FAR_LOOK)
        if t + OWN_LOOK < pairs:
            inner.append(("own", t + OWN_LOOK, 1))
        inner.append(("base", t + 1, 0))
        if t == pairs - 1:
            inner += [("base", k, 0) for k in range(pairs + 1, count - 1)]
        both = []
        if t >= 2 * LAG:
            both.append(("last", t - 2 * LAG, 0))
        if t >= LAG:
            both += [("merge", (t - LAG) * PER, PER), ("leaf", t - LAG, 0)]
        both.append(("settle", t * PER, PER))
        inner += both
        outer += both
    for k in range(pairs + FAR_LOOK, count):
        inner += far(k)
    for steps, order in ((inner, INNER), (outer, OUTER)):
        for what, i in order:
            steps.append((what, *unit(i)) if what in ("settle", "merge") else (what, pairs + i, 0))
    return inner, outer


def encode(what, a, n):
    return (OPS.index(what) * 128 + a) * 4 + (n if what in ("own", "far") else n // 2)


def words(steps):
    codes = [encode(*step) for step in steps]
    codes += [0] * (len(codes) % 2)
    return [codes[i] + STEP * codes[i + 1] for i in range(0, len(codes), 2)]


def pick(table, i):
    word = table[0]
    for k in range(1, len(table)):
        word = jnp.where(i >= k, table[k], word)
    return word


def kernel(
    rhs, leaf_v, leaf_t, merge_v, merge_t, x,
    sent, got, over, xu, mv, mt, lv, lt, far, v2, vt2, far_v2, far_vt2, l2, lt2, base_w, cross_w, merge_w, leaf_w,
    up_sem, low_sem, mv_sem, mt_sem, lv_sem, lt_sem, leaf_send, leaf_recv, far_send, far_recv, over_send, over_recv,
    send_sem, recv_sem,
):
    levels, width = merge_v.shape[0], leaf_t.shape[1]
    chunks = x.shape[0]
    pieces = sent.shape[1]
    last_level = levels - 1
    depth = lax.axis_size("rows").bit_length() - 1
    row, col = lax.axis_index("rows"), lax.axis_index("cols")
    partners, bits = [], []
    for j in range(levels):
        stride = 1 << (depth - 1 - j)
        bits.append((row // stride) % 2)
        partners.append(row + stride * (1 - 2 * bits[j]))
    beside = partners[1]
    across = partners[0] + partners[1] - row
    inner = bits[0] != bits[1]
    outer = bits[0] == bits[1]

    def columns(c):
        return pl.ds(pl.multiple_of(c * WIDTH, WIDTH), WIDTH)

    def upper_copy(c):
        return pltpu.make_async_copy(rhs.at[pl.ds(0, width), columns(c)], x.at[c, pl.ds(0, width)], up_sem.at[c])

    def lower_copy(c):
        low = pl.ds(width, x.shape[1] - width)
        return pltpu.make_async_copy(rhs.at[low, columns(c)], x.at[c, low], low_sem.at[c])

    def move(slot, p, device):
        return pltpu.make_async_remote_copy(
            src_ref=sent.at[slot, p], dst_ref=got.at[slot, p],
            send_sem=send_sem.at[slot, p], recv_sem=recv_sem.at[slot, p],
            device_id=(device, col), device_id_type=MESH,
        )

    def cross(slot, p):
        return move(slot, p, across)

    def hand_over(c):
        return pltpu.make_async_remote_copy(
            src_ref=x.at[c, pl.ds(0, width)], dst_ref=over.at[c],
            send_sem=over_send.at[c], recv_sem=over_recv.at[c],
            device_id=(beside, col), device_id_type=MESH,
        )

    def hand_back(p):
        return move(2, p, beside)

    def exchange(j, p):
        return move(j + 1, p, partners[j])

    half = leaf_v.shape[0]
    own_half = pl.ds(pl.multiple_of(col * half, half), half)
    leaf_here = pltpu.make_async_copy(leaf_v, lv.at[own_half], lv_sem)
    leaf_there = pltpu.make_async_remote_copy(
        src_ref=leaf_v, dst_ref=lv.at[own_half], send_sem=leaf_send, recv_sem=leaf_recv,
        device_id=(row, 1 - col), device_id_type=MESH,
    )
    lt_copy = pltpu.make_async_copy(leaf_t, lt, lt_sem)

    def mv_copy(j):
        return pltpu.make_async_copy(merge_v.at[j], mv.at[j], mv_sem.at[j])

    def mt_copy(j):
        return pltpu.make_async_copy(merge_t.at[j], mt.at[j], mt_sem.at[j])

    share = width // lax.axis_size("cols")
    own_share = pl.ds(pl.multiple_of(col * share, share), share)
    far_copies = [
        pltpu.make_async_remote_copy(
            src_ref=src, dst_ref=far.at[i, own_share], send_sem=far_send.at[i], recv_sem=far_recv.at[i],
            device_id=(beside, col), device_id_type=MESH,
        )
        for i, src in enumerate((merge_v.at[0, own_share], merge_t.at[0, own_share], merge_v.at[1, own_share]))
    ]
    pass_on = [
        pltpu.make_async_remote_copy(
            src_ref=far.at[i, own_share], dst_ref=far.at[i, own_share], send_sem=far_send.at[3 + i],
            recv_sem=far_recv.at[3 + i], device_id=(row, 1 - col), device_id_type=MESH,
        )
        for i in range(3)
    ]

    mv_copy(0).start()
    barrier = pltpu.get_barrier_semaphore()
    for device in [across, beside] + partners[2:]:
        pl.semaphore_signal(barrier, inc=1, device_id=(device, col), device_id_type=MESH)
    pl.semaphore_signal(barrier, inc=1, device_id=(row, 1 - col), device_id_type=MESH)

    def each(count, act, first=0):
        def one(i, carry):
            act(i)
            return carry

        lax.fori_loop(first, count, one, 0)

    each(chunks, lambda c: upper_copy(c).start())
    each(levels, lambda j: mt_copy(j).start())
    each(levels, lambda j: mv_copy(j).start(), 1)
    leaf_here.start()
    lt_copy.start()
    each(chunks, lambda c: lower_copy(c).start())

    pairs = chunks // 2 - len(TAIL)
    plans = schedule(pairs)
    tables = [words(steps) for steps in plans]

    def prepare_v(j):
        mv_copy(j).wait()
        v = mv[j]
        vt2[j] = split(v.T)
        v2[j] = split(v)

    def prepare_t(j):
        mt_copy(j).wait()
        mv[j] = times(v2.at[j], mt[j])
        v2[j] = split(mv[j])

    def receive_far(i):
        far_copies[i].wait_recv()
        pass_on[i].start()
        pass_on[i].wait()

    def far_level(j):
        v = far[2 * j]
        far_vt2[j] = split(v.T)
        far_v2[j] = split(v)

    def ready(a, n):
        each(levels, prepare_v, 1)
        each(levels, prepare_t)
        merge_w[:width] = split(times(vt2.at[3], mv[2]))
        merge_w[width:] = v2[2]
        leaf_here.wait()
        lt_copy.wait()
        leaf_there.wait()
        whole = lv[...]
        l2[...] = split(whole)
        l2[...] = split(times(l2, lt[...]))
        lt2[...] = split(whole.T)
        last = jnp.concatenate([mv[last_level], jnp.zeros((whole.shape[0] - width, width), jnp.float32)], axis=0)
        leaf_w[...] = split(last - times(l2, times(lt2, last)))

    def near(a, n):
        receive_far(0)
        far_level(0)

    def rest(a, n):
        receive_far(1)
        far[0] = times(far_v2.at[0], far[1])
        receive_far(2)
        far_level(1)
        far_v2[1] = split(times(far_v2.at[1], mt[1]))
        eye = jnp.eye(width, dtype=jnp.float32)
        onward = jnp.concatenate([unsplit(far_vt2[1]), unsplit(vt2[1])], axis=1)
        back, here = times(far_v2.at[1], onward), times(v2.at[1], onward)
        back = jnp.concatenate([eye - back[:, :width], -back[:, width:]], axis=1)
        here = jnp.concatenate([-here[:, :width], eye - here[:, width:]], axis=1)
        base_w[0] = split(back)
        base_w[1] = split(times(vt2.at[2], here))
        base_w[2] = split(here)

        def across_w(i):
            w = base_w[i]
            parts = []
            for k, v in enumerate((far[0], mv[0])):
                cut = [w[:, (2 * s + k) * width : (2 * s + k + 1) * width] for s in range(3)]
                parts.append(product(jnp.concatenate(cut, axis=1), v))
            cross_w[i] = split(jnp.concatenate(parts, axis=1))

        each(3, across_w)

    def span(p, n, act):
        act(p, 0)
        for i in range(1, PER):
            if isinstance(n, range):
                act(p + i, i)
                continue

            @pl.when(n[i] == i)
            def _():
                act(p + i, i)

    def spots(p, n):
        return [p + n[i] for i in range(PER)]

    def both(slot_a, slot_b, p, n):
        return unpack([sent[slot_a, s] + got[slot_b, s] for s in spots(p, n)])

    def put(ref, value, p, n):
        parts = pack(value)

        def act(q, i):
            ref[q] = parts[i]

        span(p, n, act)

    def take(ref, value, p, n):
        parts = pack(value)

        def act(q, i):
            ref[q] = ref[q] - parts[i]

        span(p, n, act)

    def chunk_pair(ref, k):
        return jnp.concatenate([ref[2 * k + i, :width] for i in range(2)], axis=1)

    def own(k, send):
        for i in range(2):
            upper_copy(2 * k + i).wait()
        put(sent.at[0], times(vt2.at[0], chunk_pair(x, k)), PER * k, range(PER))

        @pl.when(send == 1)
        def _():
            for i in range(PER):
                cross(0, PER * k + i).start()

    def far_stage(k, together):
        for i in range(2):
            hand_over(2 * k + i).wait_recv()
        put(sent.at[1], times(far_vt2.at[0], chunk_pair(over, k)), PER * k, range(PER))
        for i in range(PER):

            @pl.when(together == 1)
            def _():
                cross(0, PER * k + i).start()

            cross(1, PER * k + i).start()

    def base(k, n):
        news = stacked(jnp.concatenate([chunk_pair(over, k), chunk_pair(x, k)], axis=0))
        for i, ref in enumerate((sent.at[2], sent.at[3], xu)):
            put(ref, jnp.dot(base_w[i], news, preferred_element_type=jnp.float32), PER * k, range(PER))

    def crossed(p, n):
        def arrive(q, i):
            cross(0, q).wait_recv()
            cross(1, q).wait_recv()

        span(p, n, arrive)
        news = stacked(jnp.concatenate([both(1, 0, p, n), both(0, 1, p, n)], axis=0))

        def add(i):
            return jnp.dot(cross_w[i], news, preferred_element_type=jnp.float32)

        take(sent.at[2], add(0), p, n)
        span(p, n, lambda q, i: hand_back(q).start())
        take(sent.at[3], add(1), p, n)
        span(p, n, lambda q, i: exchange(2, q).start())
        take(xu, add(2), p, n)

    def take_back(p, n):
        span(p, n, lambda q, i: hand_back(q).wait_recv())
        put(sent.at[3], times(vt2.at[2], unpack([got[2, s] for s in spots(p, n)])), p, n)
        span(p, n, lambda q, i: exchange(2, q).start())

        def keep(q, i):
            xu[q] = got[2, q]

        span(p, n, keep)

    def settle(p, n):
        @pl.when(inner)
        def _():
            crossed(p, n)

        @pl.when(outer)
        def _():
            take_back(p, n)

        put(sent.at[4], times(vt2.at[3], unpack([xu[s] for s in spots(p, n)])), p, n)

    def merge(p, n):
        span(p, n, lambda q, i: exchange(2, q).wait_recv())
        delta = times(merge_w, both(3, 3, p, n))
        take(sent.at[4], delta[:width], p, n)
        span(p, n, lambda q, i: exchange(3, q).start())
        take(xu, delta[width:], p, n)

    def leaf(k, n):
        for i in range(2):
            lower_copy(2 * k + i).wait()

            @pl.when(outer)
            def _():
                hand_over(2 * k + i).wait_send()

        upper = unpack([xu[PER * k + i] for i in range(PER)])
        low = jnp.concatenate([x[2 * k + i, width:] for i in range(2)], axis=1)
        block = jnp.concatenate([upper, low], axis=0)
        block = block - times(l2, times(lt2, block))
        for i in range(2):
            x[2 * k + i] = block[:, i * WIDTH : (i + 1) * WIDTH]

    def last(k, n):
        for i in range(PER):
            exchange(last_level, PER * k + i).wait_recv()
        delta = times(leaf_w, unpack([sent[4, PER * k + i] + got[4, PER * k + i] for i in range(PER)]))
        for i in range(2):
            x[2 * k + i] = x[2 * k + i] - delta[:, i * WIDTH : (i + 1) * WIDTH]

    prepare_v(0)
    pl.semaphore_wait(barrier, levels + 1)

    def give(c):
        upper_copy(c).wait()
        hand_over(c).start()

    @pl.when(outer)
    def _():
        far_copies[0].start()
        each(4, give)
        far_copies[1].start()
        far_copies[2].start()
        each(chunks, give, 4)

    leaf_there.start()

    stages = (own, far_stage, base, settle, merge, leaf, last, ready, near, rest)

    def step(t):
        word = jnp.where(inner, *[pick(table, lax.div(t, 2)) for table in tables])
        entry = jnp.where(lax.rem(t, 2) == 0, lax.rem(word, STEP), lax.div(word, STEP))
        op, a, n = lax.div(entry, 512), lax.rem(lax.div(entry, 4), 128), lax.rem(entry, 4)
        slots = [0, lax.div(n + 1, 2), 2 * lax.div(n, 2), n + lax.div(n, 2)]
        for i, stage in enumerate(stages):

            @pl.when(op == i)
            def _():
                stage(a, slots if stage in (settle, merge) else n)

    each(jnp.where(inner, *[len(steps) for steps in plans]), step)

    @pl.when(inner)
    def _():
        def drain_inner(p):
            cross(0, p).wait_send()
            cross(1, p).wait_send()
            hand_back(p).wait_send()

        each(pieces, drain_inner)

    @pl.when(outer)
    def _():
        for copy in far_copies:
            copy.wait_send()

    def drain(p):
        for j in range(2, levels):
            exchange(j, p).wait_send()

    each(pieces, drain)


def store(x, out, sem):
    copies = [
        pltpu.make_async_copy(x.at[c], out.at[:, pl.ds(c * WIDTH, WIDTH)], sem.at[c]) for c in range(x.shape[0])
    ]
    for copy in copies:
        copy.start()
    for copy in copies:
        copy.wait()


def body(rhs, leaf_v, leaf_t, merge_v, merge_t):
    rows, cols = rhs.shape
    levels, width = merge_v.shape[0], leaf_t.shape[1]
    assert levels == 4 and width == 2 * WIDTH
    chunks = cols // WIDTH
    pieces = cols // PIECE
    packed = width * PIECE // WIDTH
    f32, bf16 = jnp.float32, jnp.bfloat16
    dma = pltpu.SemaphoreType.DMA
    anywhere = pl.BlockSpec(memory_space=pltpu.HBM)
    x = pl.pallas_call(
        kernel,
        out_shape=pltpu.VMEM((chunks, rows, WIDTH), f32),
        in_specs=[anywhere] * 5,
        out_specs=pl.BlockSpec(memory_space=pltpu.VMEM),
        scratch_shapes=[
            pltpu.VMEM((levels + 1, pieces, packed, WIDTH), f32),
            pltpu.VMEM((levels + 1, pieces, packed, WIDTH), f32),
            pltpu.VMEM((chunks, width, WIDTH), f32),
            pltpu.VMEM((pieces, packed, WIDTH), f32),
            pltpu.VMEM((levels, width, width), f32),
            pltpu.VMEM((levels, width, width), f32),
            pltpu.VMEM((rows, width), f32),
            pltpu.VMEM((width, width), f32),
            pltpu.VMEM((3, width, width), f32),
            pltpu.VMEM((levels, width, 3 * width), bf16),
            pltpu.VMEM((levels, width, 3 * width), bf16),
            pltpu.VMEM((2, width, 3 * width), bf16),
            pltpu.VMEM((2, width, 3 * width), bf16),
            pltpu.VMEM((rows, 3 * width), bf16),
            pltpu.VMEM((width, 3 * rows), bf16),
            pltpu.VMEM((3, width, 6 * width), bf16),
            pltpu.VMEM((3, width, 6 * width), bf16),
            pltpu.VMEM((2 * width, 3 * width), bf16),
            pltpu.VMEM((rows, 3 * width), bf16),
            dma((chunks,)),
            dma((chunks,)),
            dma((levels,)),
            dma((levels,)),
            dma,
            dma,
            dma,
            dma,
            dma((6,)),
            dma((6,)),
            dma((chunks,)),
            dma((chunks,)),
            dma((levels + 1, pieces)),
            dma((levels + 1, pieces)),
        ],
        compiler_params=pltpu.CompilerParams(
            collective_id=0, has_side_effects=True, vmem_limit_bytes=54 * 1024 * 1024
        ),
    )(rhs, leaf_v, leaf_t, merge_v, merge_t)
    return pl.pallas_call(
        store,
        out_shape=jax.ShapeDtypeStruct((rows, cols), f32),
        in_specs=[pl.BlockSpec(memory_space=pltpu.VMEM)],
        out_specs=anywhere,
        scratch_shapes=[dma((chunks,))],
        compiler_params=pltpu.CompilerParams(vmem_limit_bytes=2 * 1024 * 1024),
    )(pltpu.with_memory_space_constraint(x, pltpu.VMEM))


def solution(mesh):
    return jax.shard_map(
        body,
        mesh=mesh,
        in_specs=(
            P("rows", "cols"),
            P(("rows", "cols"), None),
            P("rows", None),
            P(None, "rows", None),
            P(None, "rows", None),
        ),
        out_specs=P("rows", "cols"),
        check_vma=False,
    )
```

```python
import jax
import jax.numpy as jnp
from jax import lax
from jax.experimental import pallas as pl
from jax.experimental.pallas import tpu as pltpu
from jax.sharding import PartitionSpec as P

MESH = pl.DeviceIdType.MESH
WIDTH = 128
PIECE = 64
PER = 4
STRAIGHT = 2
OWN_LOOK = 4
FAR_LOOK = 2
LAG = 2
STEP = 8192
OPS = ("own", "far", "base", "settle", "merge", "settle_few", "merge_few", "leaf", "last", "ready", "ready_leaf", "near", "rest")
TAIL = ((128, 128), (128, 128), (64, 64, 64, 64))
INNER = (
    ("merge", -2), ("settle", 0), ("base", 2), ("last", -4), ("last", -3), ("leaf", -2),
    ("settle", 1), ("merge", -1), ("last", -2), ("merge", 0), ("settle", 2), ("merge", 1),
    ("leaf", 0), ("settle", 3), ("settle", 4), ("merge", 2), ("settle", 5), ("merge", 3),
    ("settle", 6), ("settle", 7), ("leaf", 1), ("merge", 4), ("merge", 6), ("merge", 5),
    ("merge", 7), ("leaf", -1), ("last", 0), ("last", -1), ("leaf", 2), ("last", 1),
    ("last", 2),
)
OUTER = (
    ("merge", -2), ("settle", 0), ("settle", 1), ("merge", -1), ("leaf", -2), ("last", -4),
    ("last", -3), ("settle", 2), ("leaf", -1), ("merge", 1), ("merge", 0), ("settle", 3),
    ("leaf", 0), ("merge", 2), ("settle", 4), ("settle", 5), ("last", -2), ("merge", 3),
    ("last", -1), ("settle", 6), ("merge", 5), ("settle", 7), ("merge", 4), ("merge", 6),
    ("merge", 7), ("last", 0), ("leaf", 1), ("leaf", 2), ("last", 1), ("last", 2),
)

def halves(x):
    hi = x.astype(jnp.bfloat16)
    return hi, (x - hi.astype(jnp.float32)).astype(jnp.bfloat16)


def split(w):
    hi, lo = halves(w)
    return jnp.concatenate([hi, hi, lo], axis=1)


def unsplit(w):
    n = w.shape[1] // 3
    return w[:, :n].astype(jnp.float32) + w[:, 2 * n :].astype(jnp.float32)


def stacked(x):
    hi, lo = halves(x)
    return jnp.concatenate([hi, lo, hi], axis=0)


def product(w, x):
    return jnp.dot(w, stacked(x), preferred_element_type=jnp.float32)


def times(w_ref, x):
    return product(w_ref[...], x)


def swap(a, b):
    left = lax.broadcasted_iota(jnp.int32, a.shape, 1) < PIECE
    return (
        jnp.where(left, a, pltpu.roll(b, PIECE, 1)),
        jnp.where(left, pltpu.roll(a, PIECE, 1), b),
    )


def unpack(pieces):
    columns = [jnp.concatenate(swap(*pieces[i : i + 2]), axis=0) for i in range(0, len(pieces), 2)]
    return jnp.concatenate(columns, axis=1)


def pack(value):
    rows = value.shape[0] // 2
    pieces = []
    for i in range(value.shape[1] // WIDTH):
        part = value[:, i * WIDTH : (i + 1) * WIDTH]
        pieces += swap(part[:rows], part[rows:])
    return pieces


def tail_units(pairs):
    groups, at = [], pairs * PER
    for widths in TAIL:
        groups.append([])
        for w in widths:
            groups[-1].append((at, w // PIECE))
            at += w // PIECE
    return groups


def schedule(pairs):
    starts = [unit for group in tail_units(pairs) for unit in group]

    def unit(i):
        return starts[i] if i >= 0 else ((pairs + i) * PER, PER)

    count = pairs + len(TAIL)
    inner = [("own", k, 1) for k in range(1, OWN_LOOK)]
    inner += [(what, 0, 0) for what in ("ready", "near", "far", "ready_leaf")] + [("far", 1, 0), ("rest", 0, 0), ("base", 0, 0)]
    outer = [("ready", 0, 0), ("ready_leaf", 0, 0)]

    def far(k):
        if k < pairs:
            return [("far", k, 0)]
        return [("own", k, 0), ("far", k, 1)] if k < count else []

    for t in range(pairs):
        inner += far(t + FAR_LOOK)
        if t + OWN_LOOK < pairs:
            inner.append(("own", t + OWN_LOOK, 1))
        inner.append(("base", t + 1, 0))
        if t == pairs - 1:
            inner += [("base", k, 0) for k in range(pairs + 1, count - 1)]
        both = []
        if t >= 2 * LAG:
            both.append(("last", t - 2 * LAG, 0))
        if t >= LAG:
            both += [("merge", (t - LAG) * PER, PER), ("leaf", t - LAG, 0)]
        both.append(("settle", t * PER, PER))
        inner += both
        outer += both
    for k in range(pairs + FAR_LOOK, count):
        inner += far(k)
    for steps, order in ((inner, INNER), (outer, OUTER)):
        for what, i in order:
            steps.append((what, *unit(i)) if what in ("settle", "merge") else (what, pairs + i, 0))
    return inner, outer


def encode(what, a, n):
    if what in ("settle", "merge") and n < PER:
        what, n = what + "_few", n - 1
    return (OPS.index(what) * 128 + a) * 4 + n % PER


def words(steps):
    codes = [encode(*step) for step in steps]
    codes += [0] * (len(codes) % 2)
    return [codes[i] + STEP * codes[i + 1] for i in range(0, len(codes), 2)]


def pick(table, i):
    word = table[0]
    for k in range(1, len(table)):
        word = jnp.where(i >= k, table[k], word)
    return word


def kernel(
    rhs, leaf_v, leaf_t, merge_v, merge_t, x,
    sent, got, over, xu, mv, mt, lv, lt, far, v2, vt2, far_v2, far_vt2, l2, lt2, base_w, cross_w, merge_w, leaf_w,
    up_sem, low_sem, mv_sem, mt_sem, lv_sem, lt_sem, leaf_send, leaf_recv, far_send, far_recv, over_send, over_recv,
    send_sem, recv_sem,
):
    levels, width = merge_v.shape[0], leaf_t.shape[1]
    chunks = x.shape[0]
    pieces = sent.shape[1]
    last_level = levels - 1
    depth = lax.axis_size("rows").bit_length() - 1
    row, col = lax.axis_index("rows"), lax.axis_index("cols")
    partners, bits = [], []
    for j in range(levels):
        stride = 1 << (depth - 1 - j)
        bits.append((row // stride) % 2)
        partners.append(row + stride * (1 - 2 * bits[j]))
    beside = partners[1]
    across = partners[0] + partners[1] - row
    diagonal = partners[1] + partners[2] - row
    inner = bits[0] != bits[1]
    outer = bits[0] == bits[1]

    def columns(c):
        return pl.ds(pl.multiple_of(c * WIDTH, WIDTH), WIDTH)

    def upper_copy(c):
        return pltpu.make_async_copy(rhs.at[pl.ds(0, width), columns(c)], x.at[c, pl.ds(0, width)], up_sem.at[c])

    def lower_copy(c):
        low = pl.ds(width, x.shape[1] - width)
        return pltpu.make_async_copy(rhs.at[low, columns(c)], x.at[c, low], low_sem.at[c])

    def move(slot, p, count, device):
        some = pl.ds(p, count)
        return pltpu.make_async_remote_copy(
            src_ref=sent.at[slot, some], dst_ref=got.at[slot, some],
            send_sem=send_sem.at[slot, p], recv_sem=recv_sem.at[slot, p],
            device_id=(device, col), device_id_type=MESH,
        )

    def cross(slot, p, count):
        return move(slot, p, count, across)

    def hand_over(c):
        return pltpu.make_async_remote_copy(
            src_ref=x.at[c, pl.ds(0, width)], dst_ref=over.at[c],
            send_sem=over_send.at[c], recv_sem=over_recv.at[c],
            device_id=(beside, col), device_id_type=MESH,
        )

    def hand_back(p, count):
        return move(2, p, count, beside)

    def exchange(j, p, count):
        return move(j + 1, p, count, partners[j])

    def direct(p, count):
        some = pl.ds(p, count)
        return pltpu.make_async_remote_copy(
            src_ref=sent.at[levels + 1, some], dst_ref=got.at[3, some],
            send_sem=send_sem.at[levels + 1, p], recv_sem=recv_sem.at[3, p],
            device_id=(diagonal, col), device_id_type=MESH,
        )

    half = leaf_v.shape[0]
    own_half = pl.ds(pl.multiple_of(col * half, half), half)
    leaf_here = pltpu.make_async_copy(leaf_v, lv.at[own_half], lv_sem)
    leaf_there = pltpu.make_async_remote_copy(
        src_ref=leaf_v, dst_ref=lv.at[own_half], send_sem=leaf_send, recv_sem=leaf_recv,
        device_id=(row, 1 - col), device_id_type=MESH,
    )
    lt_copy = pltpu.make_async_copy(leaf_t, lt, lt_sem)

    def mv_copy(j):
        return pltpu.make_async_copy(merge_v.at[j], mv.at[j], mv_sem.at[j])

    def mt_copy(j):
        return pltpu.make_async_copy(merge_t.at[j], mt.at[j], mt_sem.at[j])

    share = width // lax.axis_size("cols")
    own_share = pl.ds(pl.multiple_of(col * share, share), share)
    far_copies = [
        pltpu.make_async_remote_copy(
            src_ref=src, dst_ref=far.at[i, own_share], send_sem=far_send.at[i], recv_sem=far_recv.at[i],
            device_id=(beside, col), device_id_type=MESH,
        )
        for i, src in enumerate([ref.at[j, own_share] for ref, j in ((merge_v, 0), (merge_t, 0), (merge_v, 1), (merge_v, 2))])
    ]
    pass_on = [
        pltpu.make_async_remote_copy(
            src_ref=far.at[i, own_share], dst_ref=far.at[i, own_share], send_sem=far_send.at[4 + i],
            recv_sem=far_recv.at[4 + i], device_id=(row, 1 - col), device_id_type=MESH,
        )
        for i in range(4)
    ]

    mv_copy(0).start()
    barrier = pltpu.get_barrier_semaphore()
    for device in [across, beside, diagonal] + partners[2:]:
        pl.semaphore_signal(barrier, inc=1, device_id=(device, col), device_id_type=MESH)
    pl.semaphore_signal(barrier, inc=1, device_id=(row, 1 - col), device_id_type=MESH)

    def each(count, act, first=0):
        def one(i, carry):
            act(i)
            return carry

        lax.fori_loop(first, count, one, 0)

    each(chunks, lambda c: upper_copy(c).start())
    each(levels, lambda j: mt_copy(j).start())
    each(levels, lambda j: mv_copy(j).start(), 1)
    leaf_here.start()
    lt_copy.start()
    each(chunks, lambda c: lower_copy(c).start())

    pairs = chunks // 2 - len(TAIL)
    straight = pieces - STRAIGHT
    plans = schedule(pairs)
    tables = [words(steps) for steps in plans]
    tail = tail_units(pairs)

    def prepare_v(j):
        mv_copy(j).wait()
        v = mv[j]
        vt2[j] = split(v.T)
        v2[j] = split(v)

    def prepare_t(j):
        mt_copy(j).wait()
        mv[j] = times(v2.at[j], mt[j])
        v2[j] = split(mv[j])

    def receive_far(i):
        far_copies[i].wait_recv()
        pass_on[i].start()
        pass_on[i].wait()

    def far_level(j):
        v = far[2 * j]
        far_vt2[j] = split(v.T)
        far_v2[j] = split(v)

    def ready(a, n):
        each(levels, prepare_v, 1)
        each(levels, prepare_t)
        merge_w[:width] = split(times(vt2.at[3], mv[2]))
        merge_w[width:] = v2[2]

    def ready_leaf(a, n):
        leaf_here.wait()
        lt_copy.wait()
        leaf_there.wait()
        whole = lv[...]
        l2[...] = split(whole)
        l2[...] = split(times(l2, lt[...]))
        lt2[...] = split(whole.T)
        last = jnp.concatenate([mv[last_level], jnp.zeros((whole.shape[0] - width, width), jnp.float32)], axis=0)
        leaf_w[...] = split(last - times(l2, times(lt2, last)))

    def near(a, n):
        receive_far(0)
        far_level(0)

    def rest(a, n):
        receive_far(1)
        far[0] = times(far_v2.at[0], far[1])
        receive_far(2)
        far_level(1)
        far_v2[1] = split(times(far_v2.at[1], mt[1]))
        eye = jnp.eye(width, dtype=jnp.float32)
        onward = jnp.concatenate([unsplit(far_vt2[1]), unsplit(vt2[1])], axis=1)
        back, here = times(far_v2.at[1], onward), times(v2.at[1], onward)
        back = jnp.concatenate([eye - back[:, :width], -back[:, width:]], axis=1)
        here = jnp.concatenate([-here[:, :width], eye - here[:, width:]], axis=1)
        base_w[0] = split(back)
        base_w[1] = split(times(vt2.at[2], here))
        base_w[2] = split(here)
        receive_far(3)
        base_w[3] = split(product(split(far[3].T), back))

        def across_w(i):
            w = base_w[i]
            parts = []
            for k, v in enumerate((far[0], mv[0])):
                cut = [w[:, (2 * s + k) * width : (2 * s + k + 1) * width] for s in range(3)]
                parts.append(product(jnp.concatenate(cut, axis=1), v))
            cross_w[i] = split(jnp.concatenate(parts, axis=1))

        each(4, across_w)

    def span(p, n, act):
        act(p, 0)
        for i in range(1, len(n)):
            if isinstance(n, range):
                act(p + i, i)
                continue

            @pl.when(n[i] == i)
            def _():
                act(p + i, i)

    def batch(p, n, act):
        if isinstance(n, range):
            act(p, PER)
            return
        for more in range(2):

            @pl.when(n[1] == more)
            def _():
                act(p, 1 + more)

    def batches(k, act):
        @pl.when(k < pairs)
        def _():
            act(PER * k, PER)

        for i, group in enumerate(tail):

            @pl.when(k == pairs + i)
            def _():
                for p, count in group:
                    act(p, count)

    def spots(p, n):
        return [p + i for i in n]

    def both(slot_a, slot_b, p, n):
        return unpack([sent[slot_a, s] + got[slot_b, s] for s in spots(p, n)])

    def put(ref, value, p, n):
        parts = pack(value)

        def act(q, i):
            ref[q] = parts[i]

        span(p, n, act)

    def take(ref, value, p, n):
        parts = pack(value)

        def act(q, i):
            ref[q] = ref[q] - parts[i]

        span(p, n, act)

    def chunk_pair(ref, k):
        return jnp.concatenate([ref[2 * k + i, :width] for i in range(2)], axis=1)

    def own_product(k):
        for i in range(2):
            upper_copy(2 * k + i).wait()
        put(sent.at[0], times(vt2.at[0], chunk_pair(x, k)), PER * k, range(PER))

    def own(k, send):
        own_product(k)

        @pl.when(send == 1)
        def _():
            cross(0, PER * k, PER).start()

    def far_stage(k, together):
        for i in range(2):
            hand_over(2 * k + i).wait_recv()
        put(sent.at[1], times(far_vt2.at[0], chunk_pair(over, k)), PER * k, range(PER))

        def send(p, count):
            if count < PER:
                cross(0, p, count).start()
            cross(1, p, count).start()

        batches(k, send)

    def base(k, n):
        news = stacked(jnp.concatenate([chunk_pair(over, k), chunk_pair(x, k)], axis=0))

        def part(i, ref):
            put(ref, jnp.dot(base_w[i], news, preferred_element_type=jnp.float32), PER * k, range(PER))

        for i, ref in enumerate((sent.at[2], sent.at[3], xu)):
            part(i, ref)

        @pl.when(PER * (k + 1) > straight)
        def _():
            part(3, sent.at[levels + 1])

    def crossed(p, n):
        def arrive(q, count):
            cross(0, q, count).wait_recv()
            cross(1, q, count).wait_recv()

        batch(p, n, arrive)
        news = stacked(jnp.concatenate([both(1, 0, p, n), both(0, 1, p, n)], axis=0))

        def add(i):
            return jnp.dot(cross_w[i], news, preferred_element_type=jnp.float32)

        take(sent.at[2], add(0), p, n)
        batch(p, n, lambda q, count: hand_back(q, count).start())

        @pl.when(p >= straight)
        def _():
            take(sent.at[levels + 1], add(3), p, n)
            batch(p, n, lambda q, count: direct(q, count).start())

        take(sent.at[3], add(1), p, n)
        batch(p, n, lambda q, count: exchange(2, q, count).start())
        take(xu, add(2), p, n)

    def take_back(p, n):
        batch(p, n, lambda q, count: hand_back(q, count).wait_recv())
        put(sent.at[3], times(vt2.at[2], unpack([got[2, s] for s in spots(p, n)])), p, n)

        @pl.when(p < straight)
        def _():
            batch(p, n, lambda q, count: exchange(2, q, count).start())

        def keep(q, i):
            xu[q] = got[2, q]

        span(p, n, keep)

    def settle(p, n):
        @pl.when(inner)
        def _():
            crossed(p, n)

        @pl.when(outer)
        def _():
            take_back(p, n)

        put(sent.at[4], times(vt2.at[3], unpack([xu[s] for s in spots(p, n)])), p, n)

    def merge(p, n):
        batch(p, n, lambda q, count: exchange(2, q, count).wait_recv())
        delta = times(merge_w, both(3, 3, p, n))
        take(sent.at[4], delta[:width], p, n)
        batch(p, n, lambda q, count: exchange(3, q, count).start())
        take(xu, delta[width:], p, n)

    def leaf(k, n):
        for i in range(2):
            lower_copy(2 * k + i).wait()

            @pl.when(outer)
            def _():
                hand_over(2 * k + i).wait_send()

        upper = unpack([xu[PER * k + i] for i in range(PER)])
        low = jnp.concatenate([x[2 * k + i, width:] for i in range(2)], axis=1)
        block = jnp.concatenate([upper, low], axis=0)
        block = block - times(l2, times(lt2, block))
        for i in range(2):
            x[2 * k + i] = block[:, i * WIDTH : (i + 1) * WIDTH]

    def last(k, n):
        batches(k, lambda p, count: exchange(last_level, p, count).wait_recv())
        delta = times(leaf_w, unpack([sent[4, PER * k + i] + got[4, PER * k + i] for i in range(PER)]))
        for i in range(2):
            x[2 * k + i] = x[2 * k + i] - delta[:, i * WIDTH : (i + 1) * WIDTH]

    prepare_v(0)

    @pl.when(inner)
    def _():
        own_product(0)

    pl.semaphore_wait(barrier, levels + 2)

    def give(c):
        upper_copy(c).wait()
        hand_over(c).start()

    @pl.when(outer)
    def _():
        far_copies[0].start()
        each(4, give)
        far_copies[1].start()
        far_copies[2].start()
        far_copies[3].start()
        each(chunks, give, 4)

    @pl.when(inner)
    def _():
        cross(0, 0, PER).start()

    leaf_there.start()

    def whole(stage):
        return lambda p, n: stage(p, range(PER))

    def few(stage):
        return lambda p, n: stage(p, (0, n))

    stages = (
        own, far_stage, base, whole(settle), whole(merge), few(settle), few(merge), leaf, last, ready, ready_leaf, near, rest,
    )

    def step(t):
        word = jnp.where(inner, *[pick(table, lax.div(t, 2)) for table in tables])
        entry = jnp.where(lax.rem(t, 2) == 0, lax.rem(word, STEP), lax.div(word, STEP))
        op, a, n = lax.div(entry, 512), lax.rem(lax.div(entry, 4), 128), lax.rem(entry, 4)
        for i, stage in enumerate(stages):

            @pl.when(op == i)
            def _():
                stage(a, n)

    each(jnp.where(inner, *[len(steps) for steps in plans]), step)

    def every(act, few=None):
        each(pairs, lambda k: act(PER * k, PER))
        for group in tail:
            for p, count in group:
                (few or act)(p, count)

    @pl.when(inner)
    def _():
        def drain_inner(p, count):
            cross(0, p, count).wait_send()
            cross(1, p, count).wait_send()
            hand_back(p, count).wait_send()
            exchange(2, p, count).wait_send()

        def drain_few(p, count):
            drain_inner(p, count)
            if p >= straight:
                direct(p, count).wait_send()

        every(drain_inner, drain_few)

    @pl.when(outer)
    def _():
        for copy in far_copies:
            copy.wait_send()

        def drain_outer(p, count):
            exchange(2, p, count).wait_send()

        def drain_few(p, count):
            if p < straight:
                drain_outer(p, count)

        every(drain_outer, drain_few)

    every(lambda p, count: exchange(last_level, p, count).wait_send())


def store(x, out, sem):
    copies = [
        pltpu.make_async_copy(x.at[c], out.at[:, pl.ds(c * WIDTH, WIDTH)], sem.at[c]) for c in range(x.shape[0])
    ]
    for copy in copies:
        copy.start()
    for copy in copies:
        copy.wait()


def body(rhs, leaf_v, leaf_t, merge_v, merge_t):
    rows, cols = rhs.shape
    levels, width = merge_v.shape[0], leaf_t.shape[1]
    assert levels == 4 and width == 2 * WIDTH
    chunks = cols // WIDTH
    pieces = cols // PIECE
    packed = width * PIECE // WIDTH
    f32, bf16 = jnp.float32, jnp.bfloat16
    dma = pltpu.SemaphoreType.DMA
    anywhere = pl.BlockSpec(memory_space=pltpu.HBM)
    x = pl.pallas_call(
        kernel,
        out_shape=pltpu.VMEM((chunks, rows, WIDTH), f32),
        in_specs=[anywhere] * 5,
        out_specs=pl.BlockSpec(memory_space=pltpu.VMEM),
        scratch_shapes=[
            pltpu.VMEM((levels + 2, pieces, packed, WIDTH), f32),
            pltpu.VMEM((levels + 1, pieces, packed, WIDTH), f32),
            pltpu.VMEM((chunks, width, WIDTH), f32),
            pltpu.VMEM((pieces, packed, WIDTH), f32),
            pltpu.VMEM((levels, width, width), f32),
            pltpu.VMEM((levels, width, width), f32),
            pltpu.VMEM((rows, width), f32),
            pltpu.VMEM((width, width), f32),
            pltpu.VMEM((4, width, width), f32),
            pltpu.VMEM((levels, width, 3 * width), bf16),
            pltpu.VMEM((levels, width, 3 * width), bf16),
            pltpu.VMEM((2, width, 3 * width), bf16),
            pltpu.VMEM((2, width, 3 * width), bf16),
            pltpu.VMEM((rows, 3 * width), bf16),
            pltpu.VMEM((width, 3 * rows), bf16),
            pltpu.VMEM((4, width, 6 * width), bf16),
            pltpu.VMEM((4, width, 6 * width), bf16),
            pltpu.VMEM((2 * width, 3 * width), bf16),
            pltpu.VMEM((rows, 3 * width), bf16),
            dma((chunks,)),
            dma((chunks,)),
            dma((levels,)),
            dma((levels,)),
            dma,
            dma,
            dma,
            dma,
            dma((8,)),
            dma((8,)),
            dma((chunks,)),
            dma((chunks,)),
            dma((levels + 2, pieces)),
            dma((levels + 1, pieces)),
        ],
        compiler_params=pltpu.CompilerParams(
            collective_id=0, has_side_effects=True, vmem_limit_bytes=54 * 1024 * 1024
        ),
    )(rhs, leaf_v, leaf_t, merge_v, merge_t)
    return pl.pallas_call(
        store,
        out_shape=jax.ShapeDtypeStruct((rows, cols), f32),
        in_specs=[pl.BlockSpec(memory_space=pltpu.VMEM)],
        out_specs=anywhere,
        scratch_shapes=[dma((chunks,))],
        compiler_params=pltpu.CompilerParams(vmem_limit_bytes=2 * 1024 * 1024),
    )(pltpu.with_memory_space_constraint(x, pltpu.VMEM))


def solution(mesh):
    return jax.shard_map(
        body,
        mesh=mesh,
        in_specs=(
            P("rows", "cols"),
            P(("rows", "cols"), None),
            P("rows", None),
            P(None, "rows", None),
            P(None, "rows", None),
        ),
        out_specs=P("rows", "cols"),
        check_vma=False,
    )
```

```python
import jax
import jax.numpy as jnp
from jax import lax
from jax.experimental import pallas as pl
from jax.experimental.pallas import tpu as pltpu
from jax.sharding import PartitionSpec as P

MESH = pl.DeviceIdType.MESH
WIDTH = 128
PIECE = 64
PER = 4
STRAIGHT = 2
OWN_LOOK = 4
FAR_LOOK = 2
LAG = 2
STEP = 8192
OPS = ("own", "far", "base", "settle", "merge", "settle_few", "merge_few", "leaf", "last", "ready", "ready_leaf", "near", "rest")
TAIL = ((128, 128), (128, 128), (64, 64, 64, 64))
INNER = (
    ("merge", -2), ("settle", 0), ("base", 2), ("last", -4), ("last", -3), ("leaf", -2),
    ("settle", 1), ("merge", -1), ("last", -2), ("merge", 0), ("settle", 2), ("merge", 1),
    ("leaf", 0), ("settle", 3), ("settle", 4), ("merge", 2), ("settle", 5), ("merge", 3),
    ("settle", 6), ("settle", 7), ("leaf", 1), ("merge", 4), ("merge", 6), ("merge", 5),
    ("merge", 7), ("leaf", -1), ("last", 0), ("last", -1), ("leaf", 2), ("last", 1),
    ("last", 2),
)
OUTER = (
    ("merge", -2), ("settle", 0), ("settle", 1), ("merge", -1), ("leaf", -2), ("last", -4),
    ("last", -3), ("settle", 2), ("leaf", -1), ("merge", 1), ("merge", 0), ("settle", 3),
    ("leaf", 0), ("merge", 2), ("settle", 4), ("settle", 5), ("last", -2), ("merge", 3),
    ("last", -1), ("settle", 6), ("merge", 5), ("settle", 7), ("merge", 4), ("merge", 6),
    ("merge", 7), ("last", 0), ("leaf", 1), ("leaf", 2), ("last", 1), ("last", 2),
)

def halves(x):
    hi = x.astype(jnp.bfloat16)
    return hi, (x - hi.astype(jnp.float32)).astype(jnp.bfloat16)


def split(w):
    hi, lo = halves(w)
    return jnp.concatenate([hi, hi, lo], axis=1)


def unsplit(w):
    n = w.shape[1] // 3
    return w[:, :n].astype(jnp.float32) + w[:, 2 * n :].astype(jnp.float32)


def stacked(x):
    hi, lo = halves(x)
    return jnp.concatenate([hi, lo, hi], axis=0)


def product(w, x):
    return jnp.dot(w, stacked(x), preferred_element_type=jnp.float32)


def times(w_ref, x):
    return product(w_ref[...], x)


def swap(a, b):
    left = lax.broadcasted_iota(jnp.int32, a.shape, 1) < PIECE
    return (
        jnp.where(left, a, pltpu.roll(b, PIECE, 1)),
        jnp.where(left, pltpu.roll(a, PIECE, 1), b),
    )


def unpack(pieces):
    columns = [jnp.concatenate(swap(*pieces[i : i + 2]), axis=0) for i in range(0, len(pieces), 2)]
    return jnp.concatenate(columns, axis=1)


def pack(value):
    rows = value.shape[0] // 2
    pieces = []
    for i in range(value.shape[1] // WIDTH):
        part = value[:, i * WIDTH : (i + 1) * WIDTH]
        pieces += swap(part[:rows], part[rows:])
    return pieces


def tail_units(pairs):
    groups, at = [], pairs * PER
    for widths in TAIL:
        groups.append([])
        for w in widths:
            groups[-1].append((at, w // PIECE))
            at += w // PIECE
    return groups


def schedule(pairs):
    starts = [unit for group in tail_units(pairs) for unit in group]

    def unit(i):
        return starts[i] if i >= 0 else ((pairs + i) * PER, PER)

    count = pairs + len(TAIL)
    inner = [("own", k, 1) for k in range(1, OWN_LOOK)]
    inner += [(what, 0, 0) for what in ("ready", "near", "far", "ready_leaf")] + [("far", 1, 0), ("rest", 0, 0), ("base", 0, 0)]
    outer = [("ready", 0, 0), ("ready_leaf", 0, 0)]

    def far(k):
        if k < pairs:
            return [("far", k, 0)]
        return [("own", k, 0), ("far", k, 1)] if k < count else []

    for t in range(pairs):
        inner += far(t + FAR_LOOK)
        if t + OWN_LOOK < pairs:
            inner.append(("own", t + OWN_LOOK, 1))
        inner.append(("base", t + 1, 0))
        if t == pairs - 1:
            inner += [("base", k, 0) for k in range(pairs + 1, count - 1)]
        both = []
        if t >= 2 * LAG:
            both.append(("last", t - 2 * LAG, 0))
        if t >= LAG:
            both += [("merge", (t - LAG) * PER, PER), ("leaf", t - LAG, 0)]
        both.append(("settle", t * PER, PER))
        inner += both
        outer += both
    for k in range(pairs + FAR_LOOK, count):
        inner += far(k)
    for steps, order in ((inner, INNER), (outer, OUTER)):
        for what, i in order:
            steps.append((what, *unit(i)) if what in ("settle", "merge") else (what, pairs + i, 0))
    return inner, outer


def encode(what, a, n):
    if what in ("settle", "merge") and n < PER:
        what, n = what + "_few", n - 1
    return (OPS.index(what) * 128 + a) * 4 + n % PER


def words(steps):
    codes = [encode(*step) for step in steps]
    codes += [0] * (len(codes) % 2)
    return [codes[i] + STEP * codes[i + 1] for i in range(0, len(codes), 2)]


def pick(table, i):
    word = table[0]
    for k in range(1, len(table)):
        word = jnp.where(i >= k, table[k], word)
    return word


def kernel(
    rhs, leaf_v, leaf_t, merge_v, merge_t, x,
    sent, got, over, xu, mv, mt, lv, lt, far, v2, vt2, far_v2, far_vt2, l2, lt2, base_w, cross_w, merge_w, leaf_w,
    up_sem, low_sem, mv_sem, mt_sem, lv_sem, lt_sem, leaf_send, leaf_recv, far_send, far_recv, over_send, over_recv,
    send_sem, recv_sem,
):
    levels, width = merge_v.shape[0], leaf_t.shape[1]
    chunks = x.shape[0]
    pieces = sent.shape[1]
    last_level = levels - 1
    depth = lax.axis_size("rows").bit_length() - 1
    row, col = lax.axis_index("rows"), lax.axis_index("cols")
    partners, bits = [], []
    for j in range(levels):
        stride = 1 << (depth - 1 - j)
        bits.append((row // stride) % 2)
        partners.append(row + stride * (1 - 2 * bits[j]))
    beside = partners[1]
    across = partners[0] + partners[1] - row
    diagonal = partners[1] + partners[2] - row
    inner = bits[0] != bits[1]
    outer = bits[0] == bits[1]

    def columns(c):
        return pl.ds(pl.multiple_of(c * WIDTH, WIDTH), WIDTH)

    def upper_copy(c):
        return pltpu.make_async_copy(rhs.at[pl.ds(0, width), columns(c)], x.at[c, pl.ds(0, width)], up_sem.at[c])

    def lower_copy(c):
        low = pl.ds(width, x.shape[1] - width)
        return pltpu.make_async_copy(rhs.at[low, columns(c)], x.at[c, low], low_sem.at[c])

    def move(slot, p, count, device):
        some = pl.ds(p, count)
        return pltpu.make_async_remote_copy(
            src_ref=sent.at[slot, some], dst_ref=got.at[slot, some],
            send_sem=send_sem.at[slot, p], recv_sem=recv_sem.at[slot, p],
            device_id=(device, col), device_id_type=MESH,
        )

    def cross(slot, p, count):
        return move(slot, p, count, across)

    def hand_over(c):
        return pltpu.make_async_remote_copy(
            src_ref=x.at[c, pl.ds(0, width)], dst_ref=over.at[c],
            send_sem=over_send.at[c], recv_sem=over_recv.at[c],
            device_id=(beside, col), device_id_type=MESH,
        )

    def hand_back(p, count):
        return move(2, p, count, beside)

    def exchange(j, p, count):
        return move(j + 1, p, count, partners[j])

    def direct(p, count):
        some = pl.ds(p, count)
        return pltpu.make_async_remote_copy(
            src_ref=sent.at[levels + 1, some], dst_ref=got.at[3, some],
            send_sem=send_sem.at[levels + 1, p], recv_sem=recv_sem.at[3, p],
            device_id=(diagonal, col), device_id_type=MESH,
        )

    half = leaf_v.shape[0]
    own_half = pl.ds(pl.multiple_of(col * half, half), half)
    leaf_here = pltpu.make_async_copy(leaf_v, lv.at[own_half], lv_sem)
    leaf_there = pltpu.make_async_remote_copy(
        src_ref=leaf_v, dst_ref=lv.at[own_half], send_sem=leaf_send, recv_sem=leaf_recv,
        device_id=(row, 1 - col), device_id_type=MESH,
    )
    lt_copy = pltpu.make_async_copy(leaf_t, lt, lt_sem)

    def mv_copy(j):
        return pltpu.make_async_copy(merge_v.at[j], mv.at[j], mv_sem.at[j])

    def mt_copy(j):
        return pltpu.make_async_copy(merge_t.at[j], mt.at[j], mt_sem.at[j])

    share = width // lax.axis_size("cols")
    own_share = pl.ds(pl.multiple_of(col * share, share), share)
    far_copies = [
        pltpu.make_async_remote_copy(
            src_ref=src, dst_ref=far.at[i, own_share], send_sem=far_send.at[i], recv_sem=far_recv.at[i],
            device_id=(beside, col), device_id_type=MESH,
        )
        for i, src in enumerate([ref.at[j, own_share] for ref, j in ((merge_v, 0), (merge_t, 0), (merge_v, 1), (merge_v, 2))])
    ]
    pass_on = [
        pltpu.make_async_remote_copy(
            src_ref=far.at[i, own_share], dst_ref=far.at[i, own_share], send_sem=far_send.at[4 + i],
            recv_sem=far_recv.at[4 + i], device_id=(row, 1 - col), device_id_type=MESH,
        )
        for i in range(4)
    ]

    mv_copy(0).start()
    barrier = pltpu.get_barrier_semaphore()
    for device in [across, beside, diagonal] + partners[2:]:
        pl.semaphore_signal(barrier, inc=1, device_id=(device, col), device_id_type=MESH)
    pl.semaphore_signal(barrier, inc=1, device_id=(row, 1 - col), device_id_type=MESH)

    def each(count, act, first=0):
        def one(i, carry):
            act(i)
            return carry

        lax.fori_loop(first, count, one, 0)

    each(chunks, lambda c: upper_copy(c).start())
    each(levels, lambda j: mt_copy(j).start())
    each(levels, lambda j: mv_copy(j).start(), 1)
    leaf_here.start()
    lt_copy.start()
    each(chunks, lambda c: lower_copy(c).start())

    pairs = chunks // 2 - len(TAIL)
    straight = pieces - STRAIGHT
    plans = schedule(pairs)
    tables = [words(steps) for steps in plans]
    tail = tail_units(pairs)

    def prepare_v(j):
        mv_copy(j).wait()
        v = mv[j]
        vt2[j] = split(v.T)
        v2[j] = split(v)

    def prepare_t(j):
        mt_copy(j).wait()
        mv[j] = times(v2.at[j], mt[j])
        v2[j] = split(mv[j])

    def receive_far(i):
        far_copies[i].wait_recv()
        pass_on[i].start()
        pass_on[i].wait()

    def far_level(j):
        v = far[2 * j]
        far_vt2[j] = split(v.T)
        far_v2[j] = split(v)

    def ready(a, n):
        each(levels, prepare_v, 1)
        each(levels, prepare_t)
        merge_w[:width] = split(times(vt2.at[3], mv[2]))
        merge_w[width:] = v2[2]

    def ready_leaf(a, n):
        leaf_here.wait()
        lt_copy.wait()
        leaf_there.wait()
        whole = lv[...]
        l2[...] = split(whole)
        l2[...] = split(times(l2, lt[...]))
        lt2[...] = split(whole.T)
        last = jnp.concatenate([mv[last_level], jnp.zeros((whole.shape[0] - width, width), jnp.float32)], axis=0)
        leaf_w[...] = split(last - times(l2, times(lt2, last)))

    def near(a, n):
        receive_far(0)
        far_level(0)

    def rest(a, n):
        receive_far(1)
        far[0] = times(far_v2.at[0], far[1])
        receive_far(2)
        far_level(1)
        far_v2[1] = split(times(far_v2.at[1], mt[1]))
        eye = jnp.eye(width, dtype=jnp.float32)
        onward = jnp.concatenate([unsplit(far_vt2[1]), unsplit(vt2[1])], axis=1)
        back, here = times(far_v2.at[1], onward), times(v2.at[1], onward)
        back = jnp.concatenate([eye - back[:, :width], -back[:, width:]], axis=1)
        here = jnp.concatenate([-here[:, :width], eye - here[:, width:]], axis=1)
        base_w[0] = split(back)
        base_w[1] = split(times(vt2.at[2], here))
        base_w[2] = split(here)
        receive_far(3)
        base_w[3] = split(product(split(far[3].T), back))

        def across_w(i):
            w = base_w[i]
            parts = []
            for k, v in enumerate((far[0], mv[0])):
                cut = [w[:, (2 * s + k) * width : (2 * s + k + 1) * width] for s in range(3)]
                parts.append(product(jnp.concatenate(cut, axis=1), v))
            cross_w[i] = split(jnp.concatenate(parts, axis=1))

        each(4, across_w)

    def span(p, n, act):
        act(p, 0)
        for i in range(1, len(n)):
            if isinstance(n, range):
                act(p + i, i)
                continue

            @pl.when(n[i] == i)
            def _():
                act(p + i, i)

    def batch(p, n, act):
        if isinstance(n, range):
            act(p, PER)
            return
        for more in range(2):

            @pl.when(n[1] == more)
            def _():
                act(p, 1 + more)

    def batches(k, act):
        @pl.when(k < pairs)
        def _():
            act(PER * k, PER)

        for i, group in enumerate(tail):

            @pl.when(k == pairs + i)
            def _():
                for p, count in group:
                    act(p, count)

    def spots(p, n):
        return [p + i for i in n]

    def both(slot_a, slot_b, p, n):
        return unpack([sent[slot_a, s] + got[slot_b, s] for s in spots(p, n)])

    def put(ref, value, p, n):
        parts = pack(value)

        def act(q, i):
            ref[q] = parts[i]

        span(p, n, act)

    def take(ref, value, p, n):
        parts = pack(value)

        def act(q, i):
            ref[q] = ref[q] - parts[i]

        span(p, n, act)

    def chunk_pair(ref, k):
        return jnp.concatenate([ref[2 * k + i, :width] for i in range(2)], axis=1)

    def own_product(k):
        for i in range(2):
            upper_copy(2 * k + i).wait()
        put(sent.at[0], times(vt2.at[0], chunk_pair(x, k)), PER * k, range(PER))

    def own(k, send):
        own_product(k)

        @pl.when(send == 1)
        def _():
            cross(0, PER * k, PER).start()

    def far_stage(k, together):
        for i in range(2):
            hand_over(2 * k + i).wait_recv()
        put(sent.at[1], times(far_vt2.at[0], chunk_pair(over, k)), PER * k, range(PER))

        def send(p, count):
            if count < PER:
                cross(0, p, count).start()
            cross(1, p, count).start()

        batches(k, send)

    def base(k, n):
        news = stacked(jnp.concatenate([chunk_pair(over, k), chunk_pair(x, k)], axis=0))

        def part(i, ref):
            put(ref, jnp.dot(base_w[i], news, preferred_element_type=jnp.float32), PER * k, range(PER))

        for i, ref in enumerate((sent.at[2], sent.at[3], xu)):
            part(i, ref)

        @pl.when(PER * (k + 1) > straight)
        def _():
            part(3, sent.at[levels + 1])

    def crossed(p, n):
        def arrive(q, count):
            cross(0, q, count).wait_recv()
            cross(1, q, count).wait_recv()

        batch(p, n, arrive)
        news = stacked(jnp.concatenate([both(1, 0, p, n), both(0, 1, p, n)], axis=0))

        def add(i):
            return jnp.dot(cross_w[i], news, preferred_element_type=jnp.float32)

        take(sent.at[2], add(0), p, n)
        batch(p, n, lambda q, count: hand_back(q, count).start())

        take(sent.at[3], add(1), p, n)
        batch(p, n, lambda q, count: exchange(2, q, count).start())

        @pl.when(p >= straight)
        def _():
            take(sent.at[levels + 1], add(3), p, n)
            batch(p, n, lambda q, count: direct(q, count).start())

        take(xu, add(2), p, n)

    def take_back(p, n):
        batch(p, n, lambda q, count: hand_back(q, count).wait_recv())
        put(sent.at[3], times(vt2.at[2], unpack([got[2, s] for s in spots(p, n)])), p, n)

        @pl.when(p < straight)
        def _():
            batch(p, n, lambda q, count: exchange(2, q, count).start())

        def keep(q, i):
            xu[q] = got[2, q]

        span(p, n, keep)

    def settle(p, n):
        @pl.when(inner)
        def _():
            crossed(p, n)

        @pl.when(outer)
        def _():
            take_back(p, n)

        put(sent.at[4], times(vt2.at[3], unpack([xu[s] for s in spots(p, n)])), p, n)

    def merge(p, n):
        batch(p, n, lambda q, count: exchange(2, q, count).wait_recv())
        delta = times(merge_w, both(3, 3, p, n))
        take(sent.at[4], delta[:width], p, n)
        batch(p, n, lambda q, count: exchange(3, q, count).start())
        take(xu, delta[width:], p, n)

    def leaf(k, n):
        for i in range(2):
            lower_copy(2 * k + i).wait()

            @pl.when(outer)
            def _():
                hand_over(2 * k + i).wait_send()

        upper = unpack([xu[PER * k + i] for i in range(PER)])
        low = jnp.concatenate([x[2 * k + i, width:] for i in range(2)], axis=1)
        block = jnp.concatenate([upper, low], axis=0)
        block = block - times(l2, times(lt2, block))
        for i in range(2):
            x[2 * k + i] = block[:, i * WIDTH : (i + 1) * WIDTH]

    def last(k, n):
        batches(k, lambda p, count: exchange(last_level, p, count).wait_recv())
        delta = times(leaf_w, unpack([sent[4, PER * k + i] + got[4, PER * k + i] for i in range(PER)]))
        for i in range(2):
            x[2 * k + i] = x[2 * k + i] - delta[:, i * WIDTH : (i + 1) * WIDTH]

    prepare_v(0)

    @pl.when(inner)
    def _():
        own_product(0)

    pl.semaphore_wait(barrier, levels + 2)

    def give(c):
        upper_copy(c).wait()
        hand_over(c).start()

    @pl.when(outer)
    def _():
        far_copies[0].start()
        each(4, give)
        far_copies[1].start()
        far_copies[2].start()
        far_copies[3].start()
        each(chunks, give, 4)

    @pl.when(inner)
    def _():
        cross(0, 0, PER).start()

    leaf_there.start()

    def whole(stage):
        return lambda p, n: stage(p, range(PER))

    def few(stage):
        return lambda p, n: stage(p, (0, n))

    stages = (
        own, far_stage, base, whole(settle), whole(merge), few(settle), few(merge), leaf, last, ready, ready_leaf, near, rest,
    )

    def step(t):
        word = jnp.where(inner, *[pick(table, lax.div(t, 2)) for table in tables])
        entry = jnp.where(lax.rem(t, 2) == 0, lax.rem(word, STEP), lax.div(word, STEP))
        op, a, n = lax.div(entry, 512), lax.rem(lax.div(entry, 4), 128), lax.rem(entry, 4)
        for i, stage in enumerate(stages):

            @pl.when(op == i)
            def _():
                stage(a, n)

    each(jnp.where(inner, *[len(steps) for steps in plans]), step)

    def every(act, few=None):
        each(pairs, lambda k: act(PER * k, PER))
        for group in tail:
            for p, count in group:
                (few or act)(p, count)

    @pl.when(inner)
    def _():
        def drain_inner(p, count):
            cross(0, p, count).wait_send()
            cross(1, p, count).wait_send()
            hand_back(p, count).wait_send()
            exchange(2, p, count).wait_send()

        def drain_few(p, count):
            drain_inner(p, count)
            if p >= straight:
                direct(p, count).wait_send()

        every(drain_inner, drain_few)

    @pl.when(outer)
    def _():
        for copy in far_copies:
            copy.wait_send()

        def drain_outer(p, count):
            exchange(2, p, count).wait_send()

        def drain_few(p, count):
            if p < straight:
                drain_outer(p, count)

        every(drain_outer, drain_few)

    every(lambda p, count: exchange(last_level, p, count).wait_send())


def store(x, out, sem):
    copies = [
        pltpu.make_async_copy(x.at[c], out.at[:, pl.ds(c * WIDTH, WIDTH)], sem.at[c]) for c in range(x.shape[0])
    ]
    for copy in copies:
        copy.start()
    for copy in copies:
        copy.wait()


def body(rhs, leaf_v, leaf_t, merge_v, merge_t):
    rows, cols = rhs.shape
    levels, width = merge_v.shape[0], leaf_t.shape[1]
    assert levels == 4 and width == 2 * WIDTH
    chunks = cols // WIDTH
    pieces = cols // PIECE
    packed = width * PIECE // WIDTH
    f32, bf16 = jnp.float32, jnp.bfloat16
    dma = pltpu.SemaphoreType.DMA
    anywhere = pl.BlockSpec(memory_space=pltpu.HBM)
    x = pl.pallas_call(
        kernel,
        out_shape=pltpu.VMEM((chunks, rows, WIDTH), f32),
        in_specs=[anywhere] * 5,
        out_specs=pl.BlockSpec(memory_space=pltpu.VMEM),
        scratch_shapes=[
            pltpu.VMEM((levels + 2, pieces, packed, WIDTH), f32),
            pltpu.VMEM((levels + 1, pieces, packed, WIDTH), f32),
            pltpu.VMEM((chunks, width, WIDTH), f32),
            pltpu.VMEM((pieces, packed, WIDTH), f32),
            pltpu.VMEM((levels, width, width), f32),
            pltpu.VMEM((levels, width, width), f32),
            pltpu.VMEM((rows, width), f32),
            pltpu.VMEM((width, width), f32),
            pltpu.VMEM((4, width, width), f32),
            pltpu.VMEM((levels, width, 3 * width), bf16),
            pltpu.VMEM((levels, width, 3 * width), bf16),
            pltpu.VMEM((2, width, 3 * width), bf16),
            pltpu.VMEM((2, width, 3 * width), bf16),
            pltpu.VMEM((rows, 3 * width), bf16),
            pltpu.VMEM((width, 3 * rows), bf16),
            pltpu.VMEM((4, width, 6 * width), bf16),
            pltpu.VMEM((4, width, 6 * width), bf16),
            pltpu.VMEM((2 * width, 3 * width), bf16),
            pltpu.VMEM((rows, 3 * width), bf16),
            dma((chunks,)),
            dma((chunks,)),
            dma((levels,)),
            dma((levels,)),
            dma,
            dma,
            dma,
            dma,
            dma((8,)),
            dma((8,)),
            dma((chunks,)),
            dma((chunks,)),
            dma((levels + 2, pieces)),
            dma((levels + 1, pieces)),
        ],
        compiler_params=pltpu.CompilerParams(
            collective_id=0, has_side_effects=True, vmem_limit_bytes=54 * 1024 * 1024
        ),
    )(rhs, leaf_v, leaf_t, merge_v, merge_t)
    return pl.pallas_call(
        store,
        out_shape=jax.ShapeDtypeStruct((rows, cols), f32),
        in_specs=[pl.BlockSpec(memory_space=pltpu.VMEM)],
        out_specs=anywhere,
        scratch_shapes=[dma((chunks,))],
        compiler_params=pltpu.CompilerParams(vmem_limit_bytes=2 * 1024 * 1024),
    )(pltpu.with_memory_space_constraint(x, pltpu.VMEM))


def solution(mesh):
    return jax.shard_map(
        body,
        mesh=mesh,
        in_specs=(
            P("rows", "cols"),
            P(("rows", "cols"), None),
            P("rows", None),
            P(None, "rows", None),
            P(None, "rows", None),
        ),
        out_specs=P("rows", "cols"),
        check_vma=False,
    )
```
